32 devices in a mesh: groups: 2 (over x), slab: 8 (over z, y), pencil: 2 (over core).
Axes of the slice: x: 2, y: 2, z: 4, core: 2. Of those that a mesh axis runs over, the one named last changes fastest.
Arguments:
- fine_field: bfloat16 [128, 32, 16, 256], P('groups', 'slab', 'pencil'), parts along dimension 0, may hold values from -6 to 6
- coarse_cotangent: bfloat16 [128, 8, 4, 64], P('groups', 'slab', 'pencil'), parts along dimension 0, may hold values from -16 to 16
- first_weight: bfloat16 [64, 1728], replicated, may hold values from -0.15625 to 0.15625
- second_weight: bfloat16 [64, 1728], replicated, may hold values from -0.15625 to 0.15625
Outputs:
- fine_grad: bfloat16 [128, 32, 16, 256], P('groups', 'slab', 'pencil'), parts along dimension 0
- first_grad: float32 [128, 1728], P('groups'), parts along dimension 0
- second_grad: float32 [128, 1728], P('groups'), parts along dimension 0
The draws below stay inside these ranges and needn't reach their ends.
There are 2 independent parts, one for each index of `groups`. The reference program is written for one: setup_inputs(seed, part) draws one part's arguments, and reference() takes and returns one part's arrays. A program takes and returns all parts, laid end to end along the dimension named above; an argument that names none is the same for every part. Nothing has to cross between parts.
All inputs are finite; a program needn't handle non-finite values.
Results may differ from the reference program's by a relative error of at most 0.005.
Values may be sent and summed in bfloat16 or wider, within the bound.
A program may use at most 128 MiB of HBM per device.

```python
import jax
import jax.numpy as jnp
from jax import lax

C = 64
NX = 256
NZ = 32
NY = 16


def block_scale(key, extent, shards, least, high):
    def one(axis_at, blocks):
        draws = jax.random.uniform(jax.random.fold_in(jax.random.fold_in(key, 6), axis_at), (blocks,), jnp.float32, least / len(shards), high / len(shards))
        return jnp.repeat(jnp.exp(draws), extent[axis_at] // blocks).reshape((-1,) + (1,) * (len(extent) - axis_at - 1))

    loudness = one(*shards[0])
    for cut in shards[1:]:
        loudness = loudness * one(*cut)
    return loudness


def gaussian(rng, dims, scale, most, cuts=(), kind=jnp.bfloat16):
    values = jax.random.normal(rng, dims, jnp.float32) * scale
    if len(cuts) > 0:
        values = block_scale(rng, dims, cuts, -0.22, 0.18) * values
    return jnp.clip(values, min=-most, max=most).astype(kind)


def setup_inputs(seed: int = 0, part: int = 0) -> dict:
    arg_keys = jax.random.split(jax.random.key(seed), 5)
    part_keys = jax.random.split(jax.random.fold_in(arg_keys[4], part), 5)
    fine_field = gaussian(part_keys[0], (C, NZ, NY, NX), 1.0, 6.0, ((1, 8), (2, 2)))
    coarse_cotangent = gaussian(part_keys[1], (C, NZ // 4, NY // 4, NX // 4), 4.0, 16.0, ((1, 8), (2, 2)))
    first_weight = gaussian(arg_keys[2], (C, 27 * C), (27 * C) ** -0.5, 0.15625)
    second_weight = gaussian(arg_keys[3], (C, 27 * C), (27 * C) ** -0.5, 0.15625)
    return {"fine_field": fine_field, "coarse_cotangent": coarse_cotangent, "first_weight": first_weight, "second_weight": second_weight}


def three_loop(values, axis):
    count = values.shape[axis]
    even = lax.slice_in_dim(values, 0, count, 2, axis)
    odd = lax.slice_in_dim(values, 1, count, 2, axis)
    return [jnp.roll(odd, 1, axis), even, odd]

def patch_block(field, tap_z):
    channels = field.shape[0]
    depth = three_loop(field, 1)[tap_z]
    columns = []
    for across in three_loop(depth, 2):
        columns.extend(three_loop(across, 3))
    return jnp.stack(columns).reshape(9 * channels, -1).astype(jnp.float32)

def alternate(even, odd, axis):
    stacked = jnp.stack([even, odd], axis=axis + 1)
    shape = list(even.shape)
    shape[axis] = 2 * shape[axis]
    return stacked.reshape(shape)

def fold_loop(values, tap_axis, axis):
    first, middle, last = [lax.index_in_dim(values, tap, tap_axis, keepdims=False) for tap in range(3)]
    return alternate(middle, last + jnp.roll(first, -1, axis), axis)

def spread_back(coarse, weight):
    channels, depth, height, length = coarse.shape
    flattened = coarse.reshape(channels, -1).astype(jnp.float32)
    per_depth = []
    for tap_z in range(3):
        w_slice = weight[:, tap_z * 9 * channels:(tap_z + 1) * 9 * channels].astype(jnp.float32)
        products = jnp.dot(w_slice.T, flattened).reshape(3, 3, channels, depth, height, length)
        per_depth.append(fold_loop(products, 1, 4))
    stacked = jnp.stack(per_depth)
    along_y = fold_loop(stacked, 1, 3)
    return fold_loop(along_y, 0, 1)

def silu_slope(values):
    sig = jax.nn.sigmoid(values)
    return sig * (1.0 + values * (1.0 - sig))

def reference(fine_field, coarse_cotangent, first_weight, second_weight):
    channels = fine_field.shape[0]
    pre_act = jnp.zeros((channels, fine_field.size // (8 * channels)), jnp.float32)
    for tap_z in range(3):
        w_slice = first_weight[:, tap_z * 9 * channels:(tap_z + 1) * 9 * channels].astype(jnp.float32)
        pre_act = pre_act + jnp.dot(w_slice, patch_block(fine_field, tap_z))
    mid_shape = (channels, fine_field.shape[1] // 2, fine_field.shape[2] // 2, fine_field.shape[3] // 2)
    hidden = jax.nn.silu(pre_act).astype(jnp.bfloat16).reshape(mid_shape)
    coarse_flat = coarse_cotangent.reshape(channels, -1).astype(jnp.float32)
    second_sum = jnp.concatenate([jnp.dot(coarse_flat, patch_block(hidden, tap_z).T) for tap_z in range(3)], axis=1)
    hidden_grad = spread_back(coarse_cotangent, second_weight)
    pre_grad = (hidden_grad.reshape(channels, -1) * silu_slope(pre_act)).astype(jnp.bfloat16)
    pre_wide = pre_grad.astype(jnp.float32)
    first_sum = jnp.concatenate([jnp.dot(pre_wide, patch_block(fine_field, tap_z).T) for tap_z in range(3)], axis=1)
    fine_grad = spread_back(pre_grad.reshape(mid_shape), first_weight).astype(jnp.bfloat16)
    first_grad = first_sum / jnp.sqrt(jnp.float32(pre_act.shape[1]))
    second_grad = second_sum / jnp.sqrt(jnp.float32(coarse_flat.shape[1]))
    return (fine_grad, first_grad, second_grad)
```

```python
import functools
import math

import jax
import jax.numpy as jnp
from jax import lax
from jax.experimental import pallas as pl
from jax.experimental.pallas import tpu as pltpu
from jax.sharding import PartitionSpec as P

MESH = pl.DeviceIdType.MESH
F32, BF16 = jnp.float32, jnp.bfloat16
RS_T, AG_T = BF16, BF16
TAP = {(0, 0): 1, (1, 0): 2, (1, 1): 0}


def tap(parity, off):
    return TAP.get((parity, off))


def dot(a, b, da, db):
    return lax.dot_general(a, b, (((da,), (db,)), ((), ())), preferred_element_type=F32)


def cat(parts, axis):
    return jnp.concatenate(parts, axis=axis)


def select_matrix(rows, columns, fn):
    row = lax.broadcasted_iota(jnp.int32, (rows, columns), 0)
    col = lax.broadcasted_iota(jnp.int32, (rows, columns), 1)
    return jnp.where(fn(row, col), 1.0, 0.0).astype(BF16)


def kernel(n, npen, scales, x_hbm, cot_hbm, w1_hbm, w2_hbm, fg_ref, g1_ref, g2_ref,
           x_ref, cot_ref, w1_ref, w2_ref, in_sem, xs, fine, corner, part_out, part_in, up, grad, hid, cs, wq, w2q, sums, xbuf, chunks, rs, ag, other,
           halo_s, halo_r, rs_s, rs_r, ag_s, ag_r, pair_s, pair_r, fwd_s, fwd_r):
    me = lax.axis_index("slab")
    pen = lax.axis_index("pencil")
    above = lax.rem(me + 1, n)
    below = lax.rem(me + n - 1, n)
    mate = lax.rem(pen + 1, npen)
    rows = 64 // n

    barrier = pltpu.get_barrier_semaphore()

    def greet(s, p):
        pl.semaphore_signal(barrier, inc=1, device_id={"slab": s, "pencil": p}, device_id_type=MESH)

    def greet_peer(d, carry):
        greet(lax.rem(me + d, n), pen)
        return carry

    lax.fori_loop(1, n, greet_peer, 0)
    greet(me, mate)
    greet(above, mate)
    greet(below, mate)

    cot_in = pltpu.make_async_copy(cot_hbm, cot_ref, in_sem.at[0])
    cot_in.start()
    x_in = []
    for b in range(4):
        at = pl.ds(b * 512, 512)
        x_in.append(pltpu.make_async_copy(x_hbm.at[at], x_ref.at[at], in_sem.at[3 + b]))
        x_in[b].start()
    w1_in = pltpu.make_async_copy(w1_hbm, w1_ref, in_sem.at[1])
    w1_in.start()
    w2_in = pltpu.make_async_copy(w2_hbm, w2_ref, in_sem.at[2])
    w2_in.start()

    def send(src, dst, k, s, p):
        copy = pltpu.make_async_remote_copy(
            src_ref=src, dst_ref=dst, send_sem=halo_s.at[k], recv_sem=halo_r.at[k],
            device_id={"slab": s, "pencil": p}, device_id_type=MESH)
        copy.start()
        return copy

    spread = select_matrix(64, 128, lambda r, c: c == 2 * r)
    cot_in.wait()
    cs[...] = dot(cot_ref[...], spread, 1, 0)
    for j in range(2):
        up[0, j, 64:128, :] = cs[pl.ds(j, 64, stride=2), :].astype(BF16)

    split = select_matrix(256, 256, lambda r, c: r == jnp.where(c < 128, 2 * c, 2 * c - 255))

    def split_block(b, carry):
        at = pl.ds(pl.multiple_of(b * 256, 256), 256)
        both = dot(x_ref[at, :], split, 1, 0)
        xs[0, at, :] = both[:, :128]
        xs[1, at, :] = both[:, 128:]
        return carry

    for b in range(4):
        x_in[b].wait()
        lax.fori_loop(2 * b, 2 * b + 2, split_block, 0)

    def plane(z, y):
        at = pl.ds(z * 8 + y, 64, stride=32)
        even, odd = xs[0, at, :], xs[1, at, :]
        fine[z, y + 1, 64:128, :] = even.astype(BF16)
        fine[z, y + 1, 128:192, :] = odd.astype(BF16)
        fine[z, y + 1, 0:64, :] = pltpu.roll(odd, 1, 1).astype(BF16)

    for y in range(8):
        plane(3, y)
    w1_in.wait()
    gap = jnp.zeros((192, 128), BF16)
    part = [cat([gap, fine[3, 1:3].reshape(384, 128)], 0)]
    part += [fine[3, 2 * j:2 * j + 3].reshape(576, 128) for j in range(1, 4)]
    part_out[...] = dot(w1_ref[:, 0:576], cat(part, 1), 1, 0).astype(BF16)
    pl.semaphore_wait(barrier, n + 2)

    halves = pl.ds(64, 128)
    middle = pl.ds(64, 64)
    part_z = send(part_out, part_in, 0, above, pen)
    fine_c = send(fine.at[3, 8, halves], corner.at[halves], 1, above, mate)
    up_z = send(up.at[0, pl.ds(0, 2), middle], up.at[1, pl.ds(0, 2), middle], 2, below, pen)
    up_y = send(up.at[0, 0, middle], up.at[0, 2, middle], 3, me, mate)
    up_c = send(up.at[0, 0, middle], up.at[1, 2, middle], 4, below, mate)

    for z in range(3):
        plane(z, 7)
    fine_y = send(fine.at[pl.ds(0, 4), 8, halves], fine.at[pl.ds(0, 4), 0, halves], 5, me, mate)
    for z in range(3):
        for y in range(7):
            plane(z, y)

    w2_in.wait()
    wq[...] = jnp.zeros_like(wq)
    w2q[...] = jnp.zeros_like(w2q)
    for a in range(2):
        for b in range(2):
            for pz in range(2):
                for py in range(2):
                    tz, ty = tap(pz, a), tap(py, b)
                    if tz is None or ty is None:
                        continue
                    for tx in range(3):
                        t = ((tz * 3 + ty) * 3 + tx) * 64
                        px, r = {1: (0, 0), 2: (1, 0), 0: (1, 1)}[tx]
                        k = ((a * 2 + b) * 2 + r) * 64
                        m = ((pz * 2 + py) * 2 + px) * 64
                        wq[k:k + 64, m:m + 64] = w1_ref[:, t:t + 64]
                        k2 = ((a * 2 + b) * 3 + tx) * 64
                        m2 = (pz * 2 + py) * 64
                        w2q[k2:k2 + 64, m2:m2 + 64] = w2_ref[:, t:t + 64]

    up_z.wait()
    up_y.wait()
    up_c.wait()
    for i in range(2):
        for j in range(3):
            mid = up[i, j, 64:128, :].astype(F32)
            up[i, j, 0:64, :] = pltpu.roll(mid, 127, 1).astype(BF16)
            up[i, j, 128:192, :] = pltpu.roll(mid, 1, 1).astype(BF16)
    rhs = cat([cat([up[a, j + b] for j in range(2)], 1) for a in range(2) for b in range(2)], 0)
    hidden_grad = dot(w2q[...], rhs, 0, 0)

    part_z.wait()
    fine_c.wait()
    fine_y.wait()

    def rim(z, y):
        odd = fine[z, y, 128:192, :].astype(F32)
        fine[z, y, 0:64, :] = pltpu.roll(odd, 1, 1).astype(BF16)

    for z in range(4):
        rim(z, 0)
    corner[0:64, :] = pltpu.roll(corner[128:192, :].astype(F32), 1, 1).astype(BF16)
    edge = dot(w1_ref[:, 0:192], corner[...], 1, 0)

    def patch(i, j, tz):
        return fine[2 * i + tz - 1, 2 * j:2 * j + 3].reshape(576, 128)

    for i in range(2):
        low = 1 - i
        taps = cat([cat([patch(i, j, tz) for j in range(4)], 1) for tz in range(low, 3)], 0)
        pre_act = dot(w1_ref[:, low * 576:], taps, 1, 0)
        for y in range(4):
            act = pre_act[:, y * 128:(y + 1) * 128]
            if i == 0:
                act = act + part_in[:, y * 128:(y + 1) * 128].astype(F32)
                act = act + edge if y == 0 else act
            sig = jax.nn.sigmoid(act)
            hid[i, y] = (act * sig).astype(BF16)
            m = (i * 2 + y % 2) * 64
            back = hidden_grad[m:m + 64, (y // 2) * 128:(y // 2 + 1) * 128]
            pre_grad = (back * (sig * (1.0 + act * (1.0 - sig)))).astype(BF16)
            grad[i, y, 0:64, :] = pre_grad
            grad[i, y, 64:128, :] = pltpu.roll(pre_grad.astype(F32), 127, 1).astype(BF16)

    low = pl.ds(0, 64)
    grad_z = send(grad.at[0, pl.ds(0, 4), low], grad.at[2, pl.ds(0, 4), low], 6, below, pen)
    grad_y = send(grad.at[pl.ds(0, 2), 0, low], grad.at[pl.ds(0, 2), 4, low], 7, me, mate)
    grad_c = send(grad.at[0, 0, low], grad.at[2, 4, low], 8, below, mate)

    pair = pltpu.make_async_remote_copy(
        src_ref=sums.at[1 - pen], dst_ref=xbuf, send_sem=pair_s.at[0], recv_sem=pair_r.at[0],
        device_id={"pencil": mate}, device_id_type=MESH)
    def rs_copy(d):
        to = lax.rem(me + d, n)
        return pltpu.make_async_remote_copy(
            src_ref=chunks.at[to], dst_ref=rs.at[d], send_sem=rs_s.at[d], recv_sem=rs_r.at[d],
            device_id={"slab": to}, device_id_type=MESH)

    def ag_copy(d):
        return pltpu.make_async_remote_copy(
            src_ref=ag.at[me], dst_ref=ag.at[me], send_sem=ag_s.at[d], recv_sem=ag_r.at[d],
            device_id={"slab": lax.rem(me + d, n)}, device_id_type=MESH)

    def ag_wait(d):
        source = lax.rem(me + n - d, n)
        pltpu.make_async_remote_copy(
            src_ref=ag.at[me], dst_ref=ag.at[source], send_sem=ag_s.at[d], recv_sem=ag_r.at[d],
            device_id={"slab": lax.rem(me + d, n)}, device_id_type=MESH).wait()

    def each(fn):
        def body(d, carry):
            fn(d)
            return carry

        lax.fori_loop(1, n, body, 0)

    def begin():
        pair.wait_recv()
        scale = jnp.where(pen == 0, scales[0], scales[1])
        total = (sums[pen] + xbuf[...]) * scale
        for s in range(n):
            chunks[s] = total[s * rows:(s + 1) * rows].astype(RS_T)
        each(lambda d: rs_copy(d).start())

    second = []
    for tz in range(3):
        i, z = {1: (0, 0), 2: (0, 1), 0: (1, 1)}[tz]
        for ty in range(3):
            at = {1: ((0, 0), (1, 2)), 2: ((0, 1), (1, 3)), 0: ((1, 1), (2, 3))}[ty]
            left = cat([up[i, j] for j, y in at], 1)
            right = cat([hid[z, y] for j, y in at], 1)
            block = dot(left, right, 1, 1)
            second.extend(block[tx * 64:(tx + 1) * 64] for tx in range(3))
    sums[1] = cat(second, 1)
    pl.when(pen == 0)(pair.start)
    pl.when(pen != 0)(begin)
    first = []
    for tz in (1, 2, 0):
        if tz == 0:
            grad_z.wait()
            grad_y.wait()
            grad_c.wait()
        span = (1, 2) if tz == 0 else (0, 1)
        cells = cat([grad[i, j, 0:64, :] for i in span for j in range(4)], 1)
        taps = cat([patch(i, j, tz) for i in span for j in range(4)], 1)
        first.append(dot(cells, taps, 1, 1))
    sums[0] = cat([first[2], first[0], first[1]], 1)


    pl.when(pen != 0)(pair.start)
    pl.when(pen == 0)(begin)
    pair.wait_send()
    for i, j in [(2, 0), (2, 1), (2, 2), (2, 3), (2, 4), (0, 4), (1, 4)]:
        here = grad[i, j, 0:64, :].astype(F32)
        grad[i, j, 64:128, :] = pltpu.roll(here, 127, 1).astype(BF16)

    for i in range(2):
        rhs = cat([cat([grad[i + a, j + b] for j in range(4)], 1) for a in range(2) for b in range(2)], 0)
        res = dot(wq[...], rhs, 0, 0)
        for pz in range(2):
            for py in range(2):
                for px in range(2):
                    m = ((pz * 2 + py) * 2 + px) * 64
                    for j in range(4):
                        at = pl.ds((2 * i + pz) * 8 + 2 * j + py, 64, stride=32)
                        xs[px, at, :] = res[m:m + 64, j * 128:(j + 1) * 128]

    each(lambda d: rs_copy(d).wait())
    mine = chunks[me].astype(F32)
    mine = lax.fori_loop(1, n, lambda d, acc: acc + rs[d].astype(F32), mine)
    ag[me] = mine.astype(AG_T)
    each(lambda d: ag_copy(d).start())

    join = select_matrix(256, 256, lambda r, c: c == jnp.where(r < 128, 2 * r, 2 * r - 255))

    def join_block(b, carry):
        at = pl.ds(pl.multiple_of(b * 256, 256), 256)
        both = cat([xs[0, at, :].astype(BF16), xs[1, at, :].astype(BF16)], 1)
        fg_ref[at, :] = dot(both, join, 1, 0).astype(BF16)
        return carry

    lax.fori_loop(0, 8, join_block, 0)

    def forward(d):
        source = lax.rem(me + n - d, n)
        return pltpu.make_async_remote_copy(
            src_ref=ag.at[source], dst_ref=other.at[source], send_sem=fwd_s.at[d], recv_sem=fwd_r.at[d],
            device_id={"pencil": mate}, device_id_type=MESH)

    def pass_on(d):
        ag_wait(d)
        forward(d).start()

    forward(0).start()
    each(pass_on)
    forward(0).wait()
    each(lambda d: forward(d).wait())
    for s in range(n):
        at = pl.ds(s * rows, rows)
        own, far = ag[s].astype(F32), other[s].astype(F32)
        g1_ref[at, :] = jnp.where(pen == 0, own, far)
        g2_ref[at, :] = jnp.where(pen == 0, far, own)


def store(fg, g1, g2, fg_hbm, g1_hbm, g2_hbm, sem):
    pairs = ((fg, fg_hbm), (g1, g1_hbm), (g2, g2_hbm))
    copies = [pltpu.make_async_copy(a, b, sem.at[k]) for k, (a, b) in enumerate(pairs)]
    for copy in copies:
        copy.start()
    for copy in copies:
        copy.wait()


def local(fine_field, coarse_cotangent, first_weight, second_weight):
    n, npen = lax.axis_size("slab"), lax.axis_size("pencil")
    members = n * npen
    scales = (1.0 / math.sqrt(1024 * members), 1.0 / math.sqrt(128 * members))
    rows = 64 // n
    vmem = pl.BlockSpec(memory_space=pltpu.VMEM)
    hbm = pl.BlockSpec(memory_space=pltpu.HBM)
    dma = pltpu.SemaphoreType.DMA
    outs = (
        jax.ShapeDtypeStruct((2048, 256), BF16),
        jax.ShapeDtypeStruct((64, 1728), F32),
        jax.ShapeDtypeStruct((64, 1728), F32),
    )
    held = (pltpu.VMEM((2048, 256), BF16), pltpu.VMEM((64, 1728), F32), pltpu.VMEM((64, 1728), F32))
    operands = (fine_field.reshape(2048, 256), coarse_cotangent.reshape(128, 64), first_weight, second_weight)
    results = pl.pallas_call(
        functools.partial(kernel, n, npen, scales),
        out_shape=held,
        in_specs=[hbm] * 4,
        out_specs=(vmem, vmem, vmem),
        scratch_shapes=[
            pltpu.VMEM((2048, 256), BF16),
            pltpu.VMEM((128, 64), BF16),
            pltpu.VMEM((64, 1728), BF16),
            pltpu.VMEM((64, 1728), BF16),
            dma((7,)),
            pltpu.VMEM((2, 2048, 128), F32),
            pltpu.VMEM((4, 9, 192, 128), BF16),
            pltpu.VMEM((192, 128), BF16),
            pltpu.VMEM((64, 512), BF16),
            pltpu.VMEM((64, 512), BF16),
            pltpu.VMEM((2, 3, 192, 128), BF16),
            pltpu.VMEM((3, 5, 128, 128), BF16),
            pltpu.VMEM((2, 4, 64, 128), BF16),
            pltpu.VMEM((128, 128), F32),
            pltpu.VMEM((512, 512), BF16),
            pltpu.VMEM((768, 256), BF16),
            pltpu.VMEM((2, 64, 1728), F32),
            pltpu.VMEM((64, 1728), F32),
            pltpu.VMEM((n, rows, 1728), RS_T),
            pltpu.VMEM((n, rows, 1728), RS_T),
            pltpu.VMEM((n, rows, 1728), AG_T),
            pltpu.VMEM((n, rows, 1728), AG_T),
            dma((9,)), dma((9,)), dma((n,)), dma((n,)), dma((n,)), dma((n,)), dma((1,)), dma((1,)), dma((n,)), dma((n,)),
        ],
        compiler_params=pltpu.CompilerParams(
            collective_id=0, has_side_effects=True, vmem_limit_bytes=40 * 1024 * 1024),
    )(*[pltpu.with_memory_space_constraint(v, pltpu.HBM) for v in operands])
    results = [pltpu.with_memory_space_constraint(v, pltpu.VMEM) for v in results]
    fine_grad, first_grad, second_grad = pl.pallas_call(
        store,
        out_shape=outs,
        in_specs=[vmem] * 3,
        out_specs=(hbm,) * 3,
        scratch_shapes=[dma((3,))],
    )(*results)
    return fine_grad.reshape(fine_field.shape), first_grad, second_grad


def solution(mesh):
    placed = (P("groups", "slab", "pencil", None), P("groups", "slab", "pencil", None), P(), P())
    return jax.shard_map(
        local,
        mesh=mesh,
        in_specs=placed,
        out_specs=(P("groups", "slab", "pencil", None), P("groups", None), P("groups", None)),
        check_vma=False,
    )
```

```python
import functools
import math

import jax
import jax.numpy as jnp
from jax import lax
from jax.experimental import pallas as pl
from jax.experimental.pallas import tpu as pltpu
from jax.sharding import PartitionSpec as P

MESH = pl.DeviceIdType.MESH
F32, BF16 = jnp.float32, jnp.bfloat16
RS_T, AG_T = BF16, BF16
TAP = {(0, 0): 1, (1, 0): 2, (1, 1): 0}


def tap(parity, off):
    return TAP.get((parity, off))


def dot(a, b, da, db):
    return lax.dot_general(a, b, (((da,), (db,)), ((), ())), preferred_element_type=F32)


def cat(parts, axis):
    return jnp.concatenate(parts, axis=axis)


def select_matrix(rows, columns, fn):
    row = lax.broadcasted_iota(jnp.int32, (rows, columns), 0)
    col = lax.broadcasted_iota(jnp.int32, (rows, columns), 1)
    return jnp.where(fn(row, col), 1.0, 0.0).astype(BF16)


def kernel(n, npen, scales, x_hbm, cot_hbm, w1_hbm, w2_hbm, fg_ref, g1_ref, g2_ref,
           x_ref, cot_ref, w1_ref, w2_ref, in_sem, xs, fine, up_out, up_in, upc_out, upc_in, up_own, down_out, down_in, downc_out, downc_in, down_own, up, grad, hid, cs, wq, w2q, sums_e, sums_l, xbuf_e, xbuf_l, chunks_e, chunks_l, rs_e, rs_l, ag_e, ag_l, other_e, other_l,
           halo_s, halo_r, rs_s, rs_r, ag_s, ag_r, pair_s, pair_r, fwd_s, fwd_r):
    me = lax.axis_index("slab")
    pen = lax.axis_index("pencil")
    above = lax.rem(me + 1, n)
    below = lax.rem(me + n - 1, n)
    mate = lax.rem(pen + 1, npen)
    rows = 64 // n

    barrier = pltpu.get_barrier_semaphore()

    def greet(s, p):
        pl.semaphore_signal(barrier, inc=1, device_id={"slab": s, "pencil": p}, device_id_type=MESH)

    def greet_peer(d, carry):
        greet(lax.rem(me + d, n), pen)
        return carry

    lax.fori_loop(1, n, greet_peer, 0)
    greet(me, mate)
    greet(above, mate)
    greet(below, mate)

    cot_in = pltpu.make_async_copy(cot_hbm, cot_ref, in_sem.at[0])
    cot_in.start()
    x_in = []
    for b in range(4):
        at = pl.ds(b * 512, 512)
        x_in.append(pltpu.make_async_copy(x_hbm.at[at], x_ref.at[at], in_sem.at[3 + b]))
        x_in[b].start()
    w1_in = pltpu.make_async_copy(w1_hbm, w1_ref, in_sem.at[1])
    w1_in.start()
    w2_in = pltpu.make_async_copy(w2_hbm, w2_ref, in_sem.at[2])
    w2_in.start()

    def send(src, dst, k, s, p):
        copy = pltpu.make_async_remote_copy(
            src_ref=src, dst_ref=dst, send_sem=halo_s.at[k], recv_sem=halo_r.at[k],
            device_id={"slab": s, "pencil": p}, device_id_type=MESH)
        copy.start()
        return copy

    spread = select_matrix(64, 128, lambda r, c: c == 2 * r)
    cot_in.wait()
    cs[...] = dot(cot_ref[...], spread, 1, 0)
    for j in range(2):
        up[0, j, 64:128, :] = cs[pl.ds(j, 64, stride=2), :].astype(BF16)

    split = select_matrix(256, 256, lambda r, c: r == jnp.where(c < 128, 2 * c, 2 * c - 255))

    def split_block(b):
        at = pl.ds(b * 256, 256)
        both = dot(x_ref[at, :], split, 1, 0)
        xs[0, at, :] = both[:, :128]
        xs[1, at, :] = both[:, 128:]

    for b in range(4):
        x_in[b].wait()
        split_block(2 * b)
        split_block(2 * b + 1)

    def plane(z, y):
        at = pl.ds(z * 8 + y, 64, stride=32)
        even, odd = xs[0, at, :], xs[1, at, :]
        fine[z, y + 1, 64:128, :] = even.astype(BF16)
        fine[z, y + 1, 128:192, :] = odd.astype(BF16)
        fine[z, y + 1, 0:64, :] = pltpu.roll(odd, 1, 1).astype(BF16)

    for y in range(8):
        plane(3, y)
    w1_in.wait()
    gap = jnp.zeros((192, 128), BF16)

    def column(z, j):
        if j == 0:
            return cat([gap, fine[z, 1:3].reshape(384, 128)], 0)
        return fine[z, 2 * j:2 * j + 3].reshape(576, 128)

    up_own[...] = dot(w1_ref[:, 0:576], cat([column(3, j) for j in range(4)], 1), 1, 0)
    up_out[...] = up_own[...].astype(BF16)
    upc_out[...] = dot(w1_ref[:, 0:192], fine[3, 8], 1, 0).astype(BF16)
    pl.semaphore_wait(barrier, n + 2)

    halves = pl.ds(64, 128)
    middle = pl.ds(64, 64)
    part_up = send(up_out, up_in, 0, above, pen)
    part_upc = send(upc_out, upc_in, 1, above, mate)
    up_z = send(up.at[0, pl.ds(0, 2), middle], up.at[1, pl.ds(0, 2), middle], 2, below, pen)
    up_y = send(up.at[0, 0, middle], up.at[0, 2, middle], 3, me, mate)
    up_c = send(up.at[0, 0, middle], up.at[1, 2, middle], 4, below, mate)

    for z in range(2):
        for y in range(8):
            plane(z, y)
    plane(2, 7)
    fine_y = send(fine.at[pl.ds(0, 4), 8, halves], fine.at[pl.ds(0, 4), 0, halves], 5, me, mate)
    down_own[...] = dot(w1_ref[:, 576:], cat([cat([column(z, j) for j in range(4)], 1) for z in range(2)], 0), 1, 0)
    down_out[...] = down_own[...].astype(BF16)
    rim_weight = cat([w1_ref[:, 576:768], w1_ref[:, 1152:1344]], 1)
    downc_out[...] = dot(rim_weight, cat([fine[0, 8], fine[1, 8]], 0), 1, 0).astype(BF16)
    part_down = send(down_out, down_in, 6, below, pen)
    part_downc = send(downc_out, downc_in, 7, below, mate)
    for y in range(7):
        plane(2, y)

    w2_in.wait()
    wq[...] = jnp.zeros_like(wq)
    w2q[...] = jnp.zeros_like(w2q)
    for a in range(2):
        for b in range(2):
            for pz in range(2):
                for py in range(2):
                    tz, ty = tap(pz, a), tap(py, b)
                    if tz is None or ty is None:
                        continue
                    for tx in range(3):
                        t = ((tz * 3 + ty) * 3 + tx) * 64
                        px, r = {1: (0, 0), 2: (1, 0), 0: (1, 1)}[tx]
                        k = ((a * 2 + b) * 2 + r) * 64
                        m = ((pz * 2 + py) * 2 + px) * 64
                        wq[k:k + 64, m:m + 64] = w1_ref[:, t:t + 64]
                        k2 = ((a * 2 + b) * 3 + tx) * 64
                        m2 = (pz * 2 + py) * 64
                        w2q[k2:k2 + 64, m2:m2 + 64] = w2_ref[:, t:t + 64]

    up_z.wait()
    up_y.wait()
    up_c.wait()
    for i in range(2):
        for j in range(3):
            mid = up[i, j, 64:128, :].astype(F32)
            up[i, j, 0:64, :] = pltpu.roll(mid, 127, 1).astype(BF16)
            up[i, j, 128:192, :] = pltpu.roll(mid, 1, 1).astype(BF16)
    rhs = cat([cat([up[a, j + b] for j in range(2)], 1) for a in range(2) for b in range(2)], 0)
    hidden_grad = dot(w2q[...], rhs, 0, 0)
    rhs = cat([cat([up[1, j + b] for j in range(2)], 1) for b in range(2)], 0)
    hidden_above = dot(w2q[0:384, 0:128], rhs, 0, 0)

    fine_y.wait()

    def rim(z, y):
        odd = fine[z, y, 128:192, :].astype(F32)
        fine[z, y, 0:64, :] = pltpu.roll(odd, 1, 1).astype(BF16)

    for z in range(4):
        rim(z, 0)

    def patch(i, j, tz):
        return fine[2 * i + tz - 1, 2 * j:2 * j + 3].reshape(576, 128)

    down_rim = dot(rim_weight, cat([fine[0, 0], fine[1, 0]], 0), 1, 0)
    up_rim = dot(w1_ref[:, 0:192], fine[3, 0], 1, 0)

    def middle_row(i, y, act):
        sig = jax.nn.sigmoid(act)
        if i < 2:
            hid[i, y] = (act * sig).astype(BF16)
        m = (i % 2 * 2 + y % 2) * 64
        back = (hidden_above if i == 2 else hidden_grad)[m:m + 64, (y // 2) * 128:(y // 2 + 1) * 128]
        pre_grad = (back * (sig * (1.0 + act * (1.0 - sig)))).astype(BF16)
        grad[i, y, 0:64, :] = pre_grad
        grad[i, y, 64:128, :] = pltpu.roll(pre_grad.astype(F32), 127, 1).astype(BF16)

    def inner_plane():
        taps = cat([cat([patch(1, j, tz) for j in range(4)], 1) for tz in range(3)], 0)
        pre_act = dot(w1_ref[...], taps, 1, 0)
        for y in range(4):
            middle_row(1, y, pre_act[:, y * 128:(y + 1) * 128])

    def face_plane(i, own, rim_own, far, rim_far):
        for y in range(4):
            at = slice(y * 128, (y + 1) * 128)
            act = own[:, at] + far[:, at].astype(F32)
            if y == 0:
                act = act + (rim_own + rim_far[...].astype(F32))
            middle_row(i, y, act)

    def each(fn):
        def body(d, carry):
            fn(d)
            return carry

        lax.fori_loop(1, n, body, 0)

    sums, xbuf, chunks = (sums_e, sums_l), (xbuf_e, xbuf_l), (chunks_e, chunks_l)
    rs, ag, other = (rs_e, rs_l), (ag_e, ag_l), (other_e, other_l)
    scale = jnp.where(pen == 0, scales[0], scales[1])

    def pair(k):
        return pltpu.make_async_remote_copy(
            src_ref=sums[k].at[1 - pen], dst_ref=xbuf[k], send_sem=pair_s.at[k], recv_sem=pair_r.at[k],
            device_id={"pencil": mate}, device_id_type=MESH)

    def rs_copy(k, d):
        to = lax.rem(me + d, n)
        return pltpu.make_async_remote_copy(
            src_ref=chunks[k].at[to], dst_ref=rs[k].at[d], send_sem=rs_s.at[k * n + d], recv_sem=rs_r.at[k * n + d],
            device_id={"slab": to}, device_id_type=MESH)

    def ag_copy(k, d, source):
        return pltpu.make_async_remote_copy(
            src_ref=ag[k].at[me], dst_ref=ag[k].at[source], send_sem=ag_s.at[k * n + d], recv_sem=ag_r.at[k * n + d],
            device_id={"slab": lax.rem(me + d, n)}, device_id_type=MESH)

    def forward(k, d):
        source = lax.rem(me + n - d, n)
        return pltpu.make_async_remote_copy(
            src_ref=ag[k].at[source], dst_ref=other[k].at[source], send_sem=fwd_s.at[k * n + d], recv_sem=fwd_r.at[k * n + d],
            device_id={"pencil": mate}, device_id_type=MESH)

    def begin(k):
        pair(k).wait_recv()
        total = (sums[k][pen] + xbuf[k][...]) * scale
        for s in range(n):
            chunks[k][s] = total[s * rows:(s + 1) * rows].astype(RS_T)
        each(lambda d: rs_copy(k, d).start())

    def finish(k):
        each(lambda d: rs_copy(k, d).wait())
        mine = chunks[k][me].astype(F32)
        mine = lax.fori_loop(1, n, lambda d, acc: acc + rs[k][d].astype(F32), mine)
        ag[k][me] = mine.astype(AG_T)
        each(lambda d: ag_copy(k, d, me).start())
        forward(k, 0).start()

    def collect(k):
        def pass_on(d):
            ag_copy(k, d, lax.rem(me + n - d, n)).wait()
            forward(k, d).start()

        each(pass_on)
        forward(k, 0).wait()
        each(lambda d: forward(k, d).wait())

    def second_block(tz, ty):
        i, z = {1: (0, 0), 2: (0, 1), 0: (1, 1)}[tz]
        at = {1: ((0, 0), (1, 2)), 2: ((0, 1), (1, 3)), 0: ((1, 1), (2, 3))}[ty]
        left = cat([up[i, j] for j, y in at], 1)
        right = cat([hid[z, y] for j, y in at], 1)
        block = dot(left, right, 1, 1)
        return [block[tx * 64:(tx + 1) * 64] for tx in range(3)]

    def first_block(tz):
        span = (1, 2) if tz == 0 else (0, 1)
        cells = cat([grad[i, j, 0:64, :] for i in span for j in range(4)], 1)
        taps = cat([patch(i, j, tz) for i in span for j in range(4)], 1)
        return dot(cells, taps, 1, 1)

    inner_plane()
    odd_taps = [t for tz in (0, 2) for ty in range(3) for t in second_block(tz, ty)]
    sums_e[1] = cat(odd_taps[:8] + odd_taps[9:], 1)
    pl.when(pen == 0)(pair(0).start)
    pl.when(pen != 0)(lambda: begin(0))
    part_up.wait()
    part_upc.wait()
    face_plane(0, down_own, down_rim, up_in, upc_in)
    part_down.wait()
    part_downc.wait()
    face_plane(2, up_own, up_rim, down_in, downc_in)

    low = pl.ds(0, 64)
    grad_y = send(grad.at[pl.ds(0, 3), 0, low], grad.at[pl.ds(0, 3), 4, low], 8, me, mate)

    sums_l[1] = cat(odd_taps[8:9] + [t for ty in range(3) for t in second_block(1, ty)], 1)
    pl.when(pen == 0)(pair(1).start)
    near = first_block(1)
    sums_e[0] = cat([near[:, 64:], first_block(2)], 1)
    pl.when(pen != 0)(pair(0).start)
    pl.when(pen == 0)(lambda: begin(0))
    pl.when(pen != 0)(lambda: begin(1))
    sums_l[0] = cat([first_block(0), near[:, :64]], 1)
    pl.when(pen != 0)(pair(1).start)
    pl.when(pen == 0)(lambda: begin(1))
    pair(0).wait_send()
    pair(1).wait_send()
    pl.when(pen != 0)(lambda: finish(0))

    grad_y.wait()
    for i, j in [(0, 4), (1, 4), (2, 4)]:
        here = grad[i, j, 0:64, :].astype(F32)
        grad[i, j, 64:128, :] = pltpu.roll(here, 127, 1).astype(BF16)

    def spread_plane(i):
        rhs = cat([cat([grad[i + a, j + b] for j in range(4)], 1) for a in range(2) for b in range(2)], 0)
        res = dot(wq[...], rhs, 0, 0)
        for pz in range(2):
            for py in range(2):
                for px in range(2):
                    m = ((pz * 2 + py) * 2 + px) * 64
                    for j in range(4):
                        at = pl.ds((2 * i + pz) * 8 + 2 * j + py, 64, stride=32)
                        xs[px, at, :] = res[m:m + 64, j * 128:(j + 1) * 128]

    spread_plane(0)
    pl.when(pen == 0)(lambda: finish(0))
    pl.when(pen != 0)(lambda: finish(1))
    spread_plane(1)
    pl.when(pen == 0)(lambda: finish(1))

    join = select_matrix(256, 256, lambda r, c: c == jnp.where(r < 128, 2 * r, 2 * r - 255))

    def join_block(b):
        at = pl.ds(b * 256, 256)
        both = cat([xs[0, at, :].astype(BF16), xs[1, at, :].astype(BF16)], 1)
        fg_ref[at, :] = dot(both, join, 1, 0).astype(BF16)

    for b in range(8):
        join_block(b)

    early = (((640, 0, 1088),), ((0, 0, 512), (1152, 512, 576)))
    late = (((0, 0, 640),), ((512, 0, 640),))
    for k, columns in ((0, early), (1, late)):
        collect(k)
        for g, g_ref in ((0, g1_ref), (1, g2_ref)):
            for s in range(n):
                at = pl.ds(s * rows, rows)
                for to, begins, size in columns[g]:
                    own, far = ag[k][s, :, begins:begins + size].astype(F32), other[k][s, :, begins:begins + size].astype(F32)
                    g_ref[at, to:to + size] = jnp.where(pen == g, own, far)


def store(fg, g1, g2, fg_hbm, g1_hbm, g2_hbm, sem):
    pairs = ((fg, fg_hbm), (g1, g1_hbm), (g2, g2_hbm))
    copies = [pltpu.make_async_copy(a, b, sem.at[k]) for k, (a, b) in enumerate(pairs)]
    for copy in copies:
        copy.start()
    for copy in copies:
        copy.wait()


def local(fine_field, coarse_cotangent, first_weight, second_weight):
    n, npen = lax.axis_size("slab"), lax.axis_size("pencil")
    members = n * npen
    scales = (1.0 / math.sqrt(1024 * members), 1.0 / math.sqrt(128 * members))
    rows = 64 // n
    widths = (1088, 640)
    vmem = pl.BlockSpec(memory_space=pltpu.VMEM)
    hbm = pl.BlockSpec(memory_space=pltpu.HBM)
    dma = pltpu.SemaphoreType.DMA
    outs = (
        jax.ShapeDtypeStruct((2048, 256), BF16),
        jax.ShapeDtypeStruct((64, 1728), F32),
        jax.ShapeDtypeStruct((64, 1728), F32),
    )
    held = (pltpu.VMEM((2048, 256), BF16), pltpu.VMEM((64, 1728), F32), pltpu.VMEM((64, 1728), F32))
    operands = (fine_field.reshape(2048, 256), coarse_cotangent.reshape(128, 64), first_weight, second_weight)
    results = pl.pallas_call(
        functools.partial(kernel, n, npen, scales),
        out_shape=held,
        in_specs=[hbm] * 4,
        out_specs=(vmem, vmem, vmem),
        scratch_shapes=[
            pltpu.VMEM((2048, 256), BF16),
            pltpu.VMEM((128, 64), BF16),
            pltpu.VMEM((64, 1728), BF16),
            pltpu.VMEM((64, 1728), BF16),
            dma((7,)),
            pltpu.VMEM((2, 2048, 128), F32),
            pltpu.VMEM((4, 9, 192, 128), BF16),
            *[pltpu.VMEM((64, 512), BF16), pltpu.VMEM((64, 512), BF16), pltpu.VMEM((64, 128), BF16), pltpu.VMEM((64, 128), BF16), pltpu.VMEM((64, 512), F32)] * 2,
            pltpu.VMEM((2, 3, 192, 128), BF16),
            pltpu.VMEM((3, 5, 128, 128), BF16),
            pltpu.VMEM((2, 4, 64, 128), BF16),
            pltpu.VMEM((128, 128), F32),
            pltpu.VMEM((512, 512), BF16),
            pltpu.VMEM((768, 256), BF16),
            *[pltpu.VMEM((2, 64, w), F32) for w in widths],
            *[pltpu.VMEM((64, w), F32) for w in widths],
            *[pltpu.VMEM((n, rows, w), RS_T) for w in widths],
            *[pltpu.VMEM((n, rows, w), RS_T) for w in widths],
            *[pltpu.VMEM((n, rows, w), AG_T) for w in widths],
            *[pltpu.VMEM((n, rows, w), AG_T) for w in widths],
            dma((9,)), dma((9,)), dma((2 * n,)), dma((2 * n,)), dma((2 * n,)), dma((2 * n,)), dma((2,)), dma((2,)), dma((2 * n,)), dma((2 * n,)),
        ],
        compiler_params=pltpu.CompilerParams(
            collective_id=0, has_side_effects=True, vmem_limit_bytes=40 * 1024 * 1024),
    )(*[pltpu.with_memory_space_constraint(v, pltpu.HBM) for v in operands])
    results = [pltpu.with_memory_space_constraint(v, pltpu.VMEM) for v in results]
    fine_grad, first_grad, second_grad = pl.pallas_call(
        store,
        out_shape=outs,
        in_specs=[vmem] * 3,
        out_specs=(hbm,) * 3,
        scratch_shapes=[dma((3,))],
    )(*results)
    return fine_grad.reshape(fine_field.shape), first_grad, second_grad


def solution(mesh):
    placed = (P("groups", "slab", "pencil", None), P("groups", "slab", "pencil", None), P(), P())
    return jax.shard_map(
        local,
        mesh=mesh,
        in_specs=placed,
        out_specs=(P("groups", "slab", "pencil", None), P("groups", None), P("groups", None)),
        check_vma=False,
    )
```

```python
import functools
import math

import jax
import jax.numpy as jnp
from jax import lax
from jax.experimental import pallas as pl
from jax.experimental.pallas import tpu as pltpu
from jax.sharding import PartitionSpec as P

MESH = pl.DeviceIdType.MESH
F32, BF16 = jnp.float32, jnp.bfloat16
RS_T, AG_T = BF16, BF16
TAP = {(0, 0): 1, (1, 0): 2, (1, 1): 0}


def tap(parity, off):
    return TAP.get((parity, off))


def dot(a, b, da, db):
    return lax.dot_general(a, b, (((da,), (db,)), ((), ())), preferred_element_type=F32)


def cat(parts, axis):
    return jnp.concatenate(parts, axis=axis)


def select_matrix(rows, columns, fn):
    row = lax.broadcasted_iota(jnp.int32, (rows, columns), 0)
    col = lax.broadcasted_iota(jnp.int32, (rows, columns), 1)
    return jnp.where(fn(row, col), 1.0, 0.0).astype(BF16)


def kernel(n, npen, scales, x_hbm, cot_hbm, w1_hbm, w2_hbm, fg_ref, g1_ref, g2_ref,
           x_ref, cot_ref, w1_ref, w2_ref, in_sem, xs, fine, up_out, up_in, upc_out, upc_in, up_own, down_out, down_in, downc_out, downc_in, down_own, inner, up, grad, hid, cs, wq, w2q, sums_e, sums_l, xbuf_e, xbuf_l, chunks_e, chunks_l, rs_e, rs_l, ag_e, ag_l, other_e, other_l,
           halo_s, halo_r, rs_s, rs_r, ag_s, ag_r, pair_s, pair_r, fwd_s, fwd_r):
    me = lax.axis_index("slab")
    pen = lax.axis_index("pencil")
    above = lax.rem(me + 1, n)
    below = lax.rem(me + n - 1, n)
    mate = lax.rem(pen + 1, npen)
    rows = 64 // n

    barrier = pltpu.get_barrier_semaphore()

    def greet(s, p):
        pl.semaphore_signal(barrier, inc=1, device_id={"slab": s, "pencil": p}, device_id_type=MESH)

    def greet_peer(d, carry):
        greet(lax.rem(me + d, n), pen)
        return carry

    cot_in = pltpu.make_async_copy(cot_hbm, cot_ref, in_sem.at[0])
    cot_in.start()
    x_in = pltpu.make_async_copy(x_hbm, x_ref, in_sem.at[3])
    x_in.start()
    w1_in = pltpu.make_async_copy(w1_hbm, w1_ref, in_sem.at[1])
    w1_in.start()
    w2_in = pltpu.make_async_copy(w2_hbm, w2_ref, in_sem.at[2])
    w2_in.start()

    lax.fori_loop(1, n, greet_peer, 0)
    greet(me, mate)
    greet(above, mate)
    greet(below, mate)

    def send(src, dst, k, s, p):
        copy = pltpu.make_async_remote_copy(
            src_ref=src, dst_ref=dst, send_sem=halo_s.at[k], recv_sem=halo_r.at[k],
            device_id={"slab": s, "pencil": p}, device_id_type=MESH)
        copy.start()
        return copy

    spread = select_matrix(64, 128, lambda r, c: c == 2 * r)
    cot_in.wait()
    cs[...] = dot(cot_ref[...], spread, 1, 0)
    for j in range(2):
        up[0, j, 64:128, :] = cs[pl.ds(j, 64, stride=2), :].astype(BF16)

    split = select_matrix(256, 256, lambda r, c: r == jnp.where(c < 128, 2 * c, 2 * c - 255))

    x_in.wait()
    both = dot(x_ref[...], split, 1, 0)
    xs[0] = both[:, :128]
    xs[1] = both[:, 128:]

    def plane(z, y):
        at = pl.ds(z * 8 + y, 64, stride=32)
        even, odd = xs[0, at, :], xs[1, at, :]
        fine[z, y + 1, 64:128, :] = even.astype(BF16)
        fine[z, y + 1, 128:192, :] = odd.astype(BF16)
        fine[z, y + 1, 0:64, :] = pltpu.roll(odd, 1, 1).astype(BF16)

    for y in range(8):
        plane(3, y)
    w1_in.wait()
    gap = jnp.zeros((192, 128), BF16)

    def column(z, j):
        if j == 0:
            return cat([gap, fine[z, 1:3].reshape(384, 128)], 0)
        return fine[z, 2 * j:2 * j + 3].reshape(576, 128)

    up_own[...] = dot(w1_ref[:, 0:576], cat([column(3, j) for j in range(4)], 1), 1, 0)
    up_out[...] = up_own[...].astype(BF16)
    upc_out[...] = dot(w1_ref[:, 0:192], fine[3, 8], 1, 0).astype(BF16)
    pl.semaphore_wait(barrier, n + 2)

    halves = pl.ds(64, 128)
    middle = pl.ds(64, 64)
    part_up = send(up_out, up_in, 0, above, pen)
    part_upc = send(upc_out, upc_in, 1, above, mate)
    up_z = send(up.at[0, pl.ds(0, 2), middle], up.at[1, pl.ds(0, 2), middle], 2, below, pen)
    up_y = send(up.at[0, 0, middle], up.at[0, 2, middle], 3, me, mate)
    up_c = send(up.at[0, 0, middle], up.at[1, 2, middle], 4, below, mate)

    for z in range(2):
        for y in range(8):
            plane(z, y)
    plane(2, 7)
    fine_y = send(fine.at[pl.ds(0, 4), 8, halves], fine.at[pl.ds(0, 4), 0, halves], 5, me, mate)
    down_own[...] = dot(w1_ref[:, 576:], cat([cat([column(z, j) for j in range(4)], 1) for z in range(2)], 0), 1, 0)
    down_out[...] = down_own[...].astype(BF16)
    rim_weight = cat([w1_ref[:, 576:768], w1_ref[:, 1152:1344]], 1)
    downc_out[...] = dot(rim_weight, cat([fine[0, 8], fine[1, 8]], 0), 1, 0).astype(BF16)
    part_down = send(down_out, down_in, 6, below, pen)
    part_downc = send(downc_out, downc_in, 7, below, mate)
    for y in range(7):
        plane(2, y)

    w2_in.wait()
    wq[...] = jnp.zeros_like(wq)
    w2q[...] = jnp.zeros_like(w2q)
    for a in range(2):
        for b in range(2):
            for pz in range(2):
                for py in range(2):
                    tz, ty = tap(pz, a), tap(py, b)
                    if tz is None or ty is None:
                        continue
                    for tx in range(3):
                        t = ((tz * 3 + ty) * 3 + tx) * 64
                        px, r = {1: (0, 0), 2: (1, 0), 0: (1, 1)}[tx]
                        k = ((a * 2 + b) * 2 + r) * 64
                        m = ((pz * 2 + py) * 2 + px) * 64
                        wq[k:k + 64, m:m + 64] = w1_ref[:, t:t + 64]
                        k2 = ((a * 2 + b) * 3 + tx) * 64
                        m2 = (pz * 2 + py) * 64
                        w2q[k2:k2 + 64, m2:m2 + 64] = w2_ref[:, t:t + 64]

    up_z.wait()
    up_y.wait()
    up_c.wait()
    for i in range(2):
        for j in range(3):
            mid = up[i, j, 64:128, :].astype(F32)
            up[i, j, 0:64, :] = pltpu.roll(mid, 127, 1).astype(BF16)
            up[i, j, 128:192, :] = pltpu.roll(mid, 1, 1).astype(BF16)
    rhs = cat([cat([up[a, j + b] for j in range(2)], 1) for a in range(2) for b in range(2)], 0)
    hidden_grad = dot(w2q[...], rhs, 0, 0)
    rhs = cat([cat([up[1, j + b] for j in range(2)], 1) for b in range(2)], 0)
    hidden_above = dot(w2q[0:384, 0:128], rhs, 0, 0)

    fine_y.wait()

    def rim(z, y):
        odd = fine[z, y, 128:192, :].astype(F32)
        fine[z, y, 0:64, :] = pltpu.roll(odd, 1, 1).astype(BF16)

    for z in range(4):
        rim(z, 0)

    def patch(i, j, tz):
        return fine[2 * i + tz - 1, 2 * j:2 * j + 3].reshape(576, 128)

    down_rim = dot(rim_weight, cat([fine[0, 0], fine[1, 0]], 0), 1, 0)
    up_rim = dot(w1_ref[:, 0:192], fine[3, 0], 1, 0)

    def middle_row(i, y, act):
        sig = jax.nn.sigmoid(act)
        if i < 2:
            hid[i, y] = (act * sig).astype(BF16)
        m = (i % 2 * 2 + y % 2) * 64
        back = (hidden_above if i == 2 else hidden_grad)[m:m + 64, (y // 2) * 128:(y // 2 + 1) * 128]
        pre_grad = (back * (sig * (1.0 + act * (1.0 - sig)))).astype(BF16)
        grad[i, y, 0:64, :] = pre_grad
        grad[i, y, 64:128, :] = pltpu.roll(pre_grad.astype(F32), 127, 1).astype(BF16)

    def inner_plane():
        taps = cat([cat([patch(1, j, tz) for j in range(4)], 1) for tz in range(3)], 0)
        pre_act = dot(w1_ref[...], taps, 1, 0)
        for y in range(4):
            middle_row(1, y, pre_act[:, y * 128:(y + 1) * 128])

    def face_plane(i, own, rim_own, far, rim_far):
        for y in range(4):
            at = slice(y * 128, (y + 1) * 128)
            act = own[:, at] + far[:, at].astype(F32)
            if y == 0:
                act = act + (rim_own + rim_far[...].astype(F32))
            middle_row(i, y, act)

    def each(fn):
        def body(d, carry):
            fn(d)
            return carry

        lax.fori_loop(1, n, body, 0)

    def far_first(fn):
        def body(k, carry):
            down, up = n - k, k - 1
            down = jnp.where(down > me, down, down - 1)
            up = jnp.where(up < me, up, up + 1)
            fn(lax.rem(jnp.where(2 * me < n, down, up) + n - me, n))
            return carry

        lax.fori_loop(1, n, body, 0)

    sums, xbuf, chunks = (sums_e, sums_l), (xbuf_e, xbuf_l), (chunks_e, chunks_l)
    rs, ag, other = (rs_e, rs_l), (ag_e, ag_l), (other_e, other_l)
    scale = jnp.where(pen == 0, scales[0], scales[1])

    def pair(k):
        return pltpu.make_async_remote_copy(
            src_ref=sums[k].at[1 - pen], dst_ref=xbuf[k], send_sem=pair_s.at[k], recv_sem=pair_r.at[k],
            device_id={"pencil": mate}, device_id_type=MESH)

    def rs_copy(k, d):
        to = lax.rem(me + d, n)
        return pltpu.make_async_remote_copy(
            src_ref=chunks[k].at[to], dst_ref=rs[k].at[d], send_sem=rs_s.at[k * n + d], recv_sem=rs_r.at[k * n + d],
            device_id={"slab": to}, device_id_type=MESH)

    def ag_copy(k, d, source):
        return pltpu.make_async_remote_copy(
            src_ref=ag[k].at[me], dst_ref=ag[k].at[source], send_sem=ag_s.at[k * n + d], recv_sem=ag_r.at[k * n + d],
            device_id={"slab": lax.rem(me + d, n)}, device_id_type=MESH)

    def forward(k, d):
        source = lax.rem(me + n - d, n)
        return pltpu.make_async_remote_copy(
            src_ref=ag[k].at[source], dst_ref=other[k].at[source], send_sem=fwd_s.at[k * n + d], recv_sem=fwd_r.at[k * n + d],
            device_id={"pencil": mate}, device_id_type=MESH)

    def begin(k):
        pair(k).wait_recv()
        total = (sums[k][pen] + xbuf[k][...]) * scale
        for s in range(n):
            chunks[k][s] = total[s * rows:(s + 1) * rows].astype(RS_T)
        far_first(lambda d: rs_copy(k, d).start())

    def finish(k):
        each(lambda d: rs_copy(k, d).wait())
        mine = chunks[k][me].astype(F32)
        mine = lax.fori_loop(1, n, lambda d, acc: acc + rs[k][d].astype(F32), mine)
        ag[k][me] = mine.astype(AG_T)
        far_first(lambda d: ag_copy(k, d, me).start())
        forward(k, 0).start()

    def collect(k):
        def pass_on(d):
            ag_copy(k, d, lax.rem(me + n - d, n)).wait()
            forward(k, d).start()

        each(pass_on)
        forward(k, 0).wait()
        each(lambda d: forward(k, d).wait())

    def second_block(tz, ty):
        i, z = {1: (0, 0), 2: (0, 1), 0: (1, 1)}[tz]
        at = {1: ((0, 0), (1, 2)), 2: ((0, 1), (1, 3)), 0: ((1, 1), (2, 3))}[ty]
        left = cat([up[i, j] for j, y in at], 1)
        right = cat([hid[z, y] for j, y in at], 1)
        block = dot(left, right, 1, 1)
        return [block[tx * 64:(tx + 1) * 64] for tx in range(3)]

    def first_block(i, tz):
        cells = cat([grad[i, j, 0:64, :] for j in range(4)], 1)
        taps = cat([patch(i, j, tz) for j in range(4)], 1)
        return dot(cells, taps, 1, 1)

    inner_plane()
    odd_taps = [t for tz in (0, 2) for ty in range(3) for t in second_block(tz, ty)]
    sums_e[1] = cat(odd_taps[:8] + odd_taps[9:], 1)
    pl.when(pen == 0)(pair(0).start)
    for tz in range(3):
        inner[tz] = first_block(1, tz)
    pl.when(pen != 0)(lambda: begin(0))
    part_up.wait()
    part_upc.wait()
    face_plane(0, down_own, down_rim, up_in, upc_in)
    part_down.wait()
    part_downc.wait()
    face_plane(2, up_own, up_rim, down_in, downc_in)

    low = pl.ds(0, 64)
    grad_y = send(grad.at[pl.ds(0, 3), 0, low], grad.at[pl.ds(0, 3), 4, low], 8, me, mate)

    sums_l[1] = cat(odd_taps[8:9] + [t for ty in range(3) for t in second_block(1, ty)], 1)
    pl.when(pen == 0)(pair(1).start)
    near = inner[1] + first_block(0, 1)
    sums_e[0] = cat([near[:, 64:], inner[2] + first_block(0, 2)], 1)
    pl.when(pen != 0)(pair(0).start)
    pl.when(pen == 0)(lambda: begin(0))
    pl.when(pen != 0)(lambda: begin(1))
    sums_l[0] = cat([inner[0] + first_block(2, 0), near[:, :64]], 1)
    pl.when(pen != 0)(pair(1).start)
    pl.when(pen == 0)(lambda: begin(1))
    pair(0).wait_send()
    pair(1).wait_send()
    grad_y.wait()
    for i, j in [(0, 4), (1, 4), (2, 4)]:
        here = grad[i, j, 0:64, :].astype(F32)
        grad[i, j, 64:128, :] = pltpu.roll(here, 127, 1).astype(BF16)

    def spread_plane(i):
        rhs = cat([cat([grad[i + a, j + b] for j in range(4)], 1) for a in range(2) for b in range(2)], 0)
        res = dot(wq[...], rhs, 0, 0)
        for pz in range(2):
            for py in range(2):
                for px in range(2):
                    m = ((pz * 2 + py) * 2 + px) * 64
                    for j in range(4):
                        at = pl.ds((2 * i + pz) * 8 + 2 * j + py, 64, stride=32)
                        xs[px, at, :] = res[m:m + 64, j * 128:(j + 1) * 128]

    join = select_matrix(256, 256, lambda r, c: c == jnp.where(r < 128, 2 * r, 2 * r - 255))

    spread_plane(0)
    spread_plane(1)
    pl.when(pen == 0)(lambda: finish(0))
    pl.when(pen == 0)(lambda: finish(1))
    both = cat([xs[0].astype(BF16), xs[1].astype(BF16)], 1)
    fg_ref[...] = dot(both, join, 1, 0).astype(BF16)

    pl.when(pen != 0)(lambda: finish(0))
    pl.when(pen != 0)(lambda: finish(1))
    early = (((640, 0, 1088),), ((0, 0, 512), (1152, 512, 576)))
    late = (((0, 0, 640),), ((512, 0, 640),))
    for k, columns in ((0, early), (1, late)):
        collect(k)
        for g, g_ref in ((0, g1_ref), (1, g2_ref)):
            for s in range(n):
                at = pl.ds(s * rows, rows)
                for to, begins, size in columns[g]:
                    own, far = ag[k][s, :, begins:begins + size].astype(F32), other[k][s, :, begins:begins + size].astype(F32)
                    g_ref[at, to:to + size] = jnp.where(pen == g, own, far)


def store(fg, g1, g2, fg_hbm, g1_hbm, g2_hbm, sem):
    pairs = ((fg, fg_hbm), (g1, g1_hbm), (g2, g2_hbm))
    copies = [pltpu.make_async_copy(a, b, sem.at[k]) for k, (a, b) in enumerate(pairs)]
    for copy in copies:
        copy.start()
    for copy in copies:
        copy.wait()


def local(fine_field, coarse_cotangent, first_weight, second_weight):
    n, npen = lax.axis_size("slab"), lax.axis_size("pencil")
    members = n * npen
    scales = (1.0 / math.sqrt(1024 * members), 1.0 / math.sqrt(128 * members))
    rows = 64 // n
    widths = (1088, 640)
    vmem = pl.BlockSpec(memory_space=pltpu.VMEM)
    hbm = pl.BlockSpec(memory_space=pltpu.HBM)
    dma = pltpu.SemaphoreType.DMA
    outs = (
        jax.ShapeDtypeStruct((2048, 256), BF16),
        jax.ShapeDtypeStruct((64, 1728), F32),
        jax.ShapeDtypeStruct((64, 1728), F32),
    )
    held = (pltpu.VMEM((2048, 256), BF16), pltpu.VMEM((64, 1728), F32), pltpu.VMEM((64, 1728), F32))
    operands = (fine_field.reshape(2048, 256), coarse_cotangent.reshape(128, 64), first_weight, second_weight)
    results = pl.pallas_call(
        functools.partial(kernel, n, npen, scales),
        out_shape=held,
        in_specs=[hbm] * 4,
        out_specs=(vmem, vmem, vmem),
        scratch_shapes=[
            pltpu.VMEM((2048, 256), BF16),
            pltpu.VMEM((128, 64), BF16),
            pltpu.VMEM((64, 1728), BF16),
            pltpu.VMEM((64, 1728), BF16),
            dma((4,)),
            pltpu.VMEM((2, 2048, 128), F32),
            pltpu.VMEM((4, 9, 192, 128), BF16),
            *[pltpu.VMEM((64, 512), BF16), pltpu.VMEM((64, 512), BF16), pltpu.VMEM((64, 128), BF16), pltpu.VMEM((64, 128), BF16), pltpu.VMEM((64, 512), F32)] * 2,
            pltpu.VMEM((3, 64, 576), F32),
            pltpu.VMEM((2, 3, 192, 128), BF16),
            pltpu.VMEM((3, 5, 128, 128), BF16),
            pltpu.VMEM((2, 4, 64, 128), BF16),
            pltpu.VMEM((128, 128), F32),
            pltpu.VMEM((512, 512), BF16),
            pltpu.VMEM((768, 256), BF16),
            *[pltpu.VMEM((2, 64, w), F32) for w in widths],
            *[pltpu.VMEM((64, w), F32) for w in widths],
            *[pltpu.VMEM((n, rows, w), RS_T) for w in widths],
            *[pltpu.VMEM((n, rows, w), RS_T) for w in widths],
            *[pltpu.VMEM((n, rows, w), AG_T) for w in widths],
            *[pltpu.VMEM((n, rows, w), AG_T) for w in widths],
            dma((9,)), dma((9,)), dma((2 * n,)), dma((2 * n,)), dma((2 * n,)), dma((2 * n,)), dma((2,)), dma((2,)), dma((2 * n,)), dma((2 * n,)),
        ],
        compiler_params=pltpu.CompilerParams(
            collective_id=0, has_side_effects=True, vmem_limit_bytes=40 * 1024 * 1024),
    )(*[pltpu.with_memory_space_constraint(v, pltpu.HBM) for v in operands])
    results = [pltpu.with_memory_space_constraint(v, pltpu.VMEM) for v in results]
    fine_grad, first_grad, second_grad = pl.pallas_call(
        store,
        out_shape=outs,
        in_specs=[vmem] * 3,
        out_specs=(hbm,) * 3,
        scratch_shapes=[dma((3,))],
    )(*results)
    return fine_grad.reshape(fine_field.shape), first_grad, second_grad


def solution(mesh):
    placed = (P("groups", "slab", "pencil", None), P("groups", "slab", "pencil", None), P(), P())
    return jax.shard_map(
        local,
        mesh=mesh,
        in_specs=placed,
        out_specs=(P("groups", "slab", "pencil", None), P("groups", None), P("groups", None)),
        check_vma=False,
    )
```

```python
import functools
import math

import jax
import jax.numpy as jnp
from jax import lax
from jax.experimental import pallas as pl
from jax.experimental.pallas import tpu as pltpu
from jax.sharding import PartitionSpec as P

MESH = pl.DeviceIdType.MESH
F32, BF16 = jnp.float32, jnp.bfloat16
RS_T, AG_T = BF16, BF16
TAP = {(0, 0): 1, (1, 0): 2, (1, 1): 0}


def tap(parity, off):
    return TAP.get((parity, off))


def dot(a, b, da, db):
    return lax.dot_general(a, b, (((da,), (db,)), ((), ())), preferred_element_type=F32)


def cat(parts, axis):
    return jnp.concatenate(parts, axis=axis)


def select_matrix(rows, columns, fn):
    row = lax.broadcasted_iota(jnp.int32, (rows, columns), 0)
    col = lax.broadcasted_iota(jnp.int32, (rows, columns), 1)
    return jnp.where(fn(row, col), 1.0, 0.0).astype(BF16)


def kernel(n, npen, scales, x_hbm, cot_hbm, w1_hbm, w2_hbm, fg_ref, g1_ref, g2_ref,
           x_ref, cot_ref, w1_ref, w2_ref, in_sem, xs, fine, up_out, up_in, up_own, down_out, down_in, down_own, inner, up, grad, hid, cs, wq, w2q, sums_0, sums_1, xbuf_0, xbuf_1, chunks_0, chunks_1, rs_0, rs_1, ag_0, ag_1, other_0, other_1,
           halo_s, halo_r, rs_s, rs_r, ag_s, ag_r, pair_s, pair_r, fwd_s, fwd_r):
    me = lax.axis_index("slab")
    pen = lax.axis_index("pencil")
    above = lax.rem(me + 1, n)
    below = lax.rem(me + n - 1, n)
    mate = lax.rem(pen + 1, npen)
    rows = 64 // n

    barrier = pltpu.get_barrier_semaphore()

    def greet(s, p):
        pl.semaphore_signal(barrier, inc=1, device_id={"slab": s, "pencil": p}, device_id_type=MESH)

    def greet_peer(d, carry):
        greet(lax.rem(me + d, n), pen)
        return carry

    cot_in = pltpu.make_async_copy(cot_hbm, cot_ref, in_sem.at[0])
    cot_in.start()
    x_in = pltpu.make_async_copy(x_hbm, x_ref, in_sem.at[3])
    x_in.start()
    w1_in = pltpu.make_async_copy(w1_hbm, w1_ref, in_sem.at[1])
    w1_in.start()
    w2_in = pltpu.make_async_copy(w2_hbm, w2_ref, in_sem.at[2])
    w2_in.start()

    lax.fori_loop(1, n, greet_peer, 0)
    greet(me, mate)
    greet(above, mate)
    greet(below, mate)

    def send(src, dst, k, s, p):
        copy = pltpu.make_async_remote_copy(
            src_ref=src, dst_ref=dst, send_sem=halo_s.at[k], recv_sem=halo_r.at[k],
            device_id={"slab": s, "pencil": p}, device_id_type=MESH)
        copy.start()
        return copy

    spread = select_matrix(64, 128, lambda r, c: c == 2 * r)
    cot_in.wait()
    cs[...] = dot(cot_ref[...], spread, 1, 0)
    for j in range(2):
        up[0, j, 64:128, :] = cs[pl.ds(j, 64, stride=2), :].astype(BF16)

    pl.semaphore_wait(barrier, n + 2)
    halves = pl.ds(64, 128)
    middle = pl.ds(64, 64)
    up_z = send(up.at[0, pl.ds(0, 2), middle], up.at[1, pl.ds(0, 2), middle], 0, below, pen)
    up_y = send(up.at[0, 0, middle], up.at[0, 2, middle], 1, me, mate)
    up_c = send(up.at[0, 0, middle], up.at[1, 2, middle], 2, below, mate)

    split = select_matrix(256, 256, lambda r, c: r == jnp.where(c < 128, 2 * c, 2 * c - 255))

    x_in.wait()
    both = dot(x_ref[...], split, 1, 0)
    xs[0] = both[:, :128]
    xs[1] = both[:, 128:]

    def plane(z, y):
        at = pl.ds(z * 8 + y, 64, stride=32)
        even, odd = xs[0, at, :], xs[1, at, :]
        fine[z, y + 1, 64:128, :] = even.astype(BF16)
        fine[z, y + 1, 128:192, :] = odd.astype(BF16)
        fine[z, y + 1, 0:64, :] = pltpu.roll(odd, 1, 1).astype(BF16)

    def rim_send(z, count, k):
        at = pl.ds(z, count)
        return send(fine.at[at, 8, halves], fine.at[at, 0, halves], k, me, mate)

    def rim(z):
        odd = fine[z, 0, 128:192, :].astype(F32)
        fine[z, 0, 0:64, :] = pltpu.roll(odd, 1, 1).astype(BF16)

    def column(z, j):
        return fine[z, 2 * j:2 * j + 3].reshape(576, 128)

    def partial_sum(own, out, landing, k, to, planes, weight, first):
        at = slice(0, 1) if first else slice(1, 4)
        taps = cat([cat([column(z, j) for j in range(4)[at]], 1) for z in planes], 0)
        res = dot(weight, taps, 1, 0)
        piece = pl.ds(0, 64) if first else pl.ds(64, 192)
        for j in range(4)[at]:
            c = res[:, (j - at.start) * 128:(j - at.start + 1) * 128]
            own[j * 64:(j + 1) * 64] = c
            out[j * 64:(j + 1) * 64] = c.astype(BF16)
        return send(out.at[piece], landing.at[piece], k, to, pen)

    plane(3, 7)
    rim_3 = rim_send(3, 1, 3)
    for y in range(7):
        plane(3, y)
    w1_in.wait()
    part_up = partial_sum(up_own, up_out, up_in, 4, above, (3,), w1_ref[:, 0:576], False)
    plane(0, 7)
    plane(1, 7)
    rim_01 = rim_send(0, 2, 5)
    for z in range(2):
        for y in range(7):
            plane(z, y)
    part_down = partial_sum(down_own, down_out, down_in, 6, below, (0, 1), w1_ref[:, 576:], False)
    plane(2, 7)
    rim_2 = rim_send(2, 1, 7)
    rim_3.wait()
    rim(3)
    part_up0 = partial_sum(up_own, up_out, up_in, 9, above, (3,), w1_ref[:, 0:576], True)
    rim_01.wait()
    rim(0)
    rim(1)
    part_down0 = partial_sum(down_own, down_out, down_in, 10, below, (0, 1), w1_ref[:, 576:], True)
    for y in range(7):
        plane(2, y)

    w2_in.wait()
    wq[...] = jnp.zeros_like(wq)
    w2q[...] = jnp.zeros_like(w2q)
    for a in range(2):
        for b in range(2):
            for pz in range(2):
                for py in range(2):
                    tz, ty = tap(pz, a), tap(py, b)
                    if tz is None or ty is None:
                        continue
                    for tx in range(3):
                        t = ((tz * 3 + ty) * 3 + tx) * 64
                        px, r = {1: (0, 0), 2: (1, 0), 0: (1, 1)}[tx]
                        k = ((a * 2 + b) * 2 + r) * 64
                        m = ((pz * 2 + py) * 2 + px) * 64
                        wq[k:k + 64, m:m + 64] = w1_ref[:, t:t + 64]
                        k2 = ((a * 2 + b) * 3 + tx) * 64
                        m2 = (pz * 2 + py) * 64
                        w2q[k2:k2 + 64, m2:m2 + 64] = w2_ref[:, t:t + 64]

    up_z.wait()
    up_y.wait()
    up_c.wait()
    for i in range(2):
        for j in range(3):
            mid = up[i, j, 64:128, :].astype(F32)
            up[i, j, 0:64, :] = pltpu.roll(mid, 127, 1).astype(BF16)
            up[i, j, 128:192, :] = pltpu.roll(mid, 1, 1).astype(BF16)
    rhs = cat([cat([up[a, j + b] for j in range(2)], 1) for a in range(2) for b in range(2)], 0)
    hidden_grad = dot(w2q[...], rhs, 0, 0)
    rhs = cat([cat([up[1, j + b] for j in range(2)], 1) for b in range(2)], 0)
    hidden_above = dot(w2q[0:384, 0:128], rhs, 0, 0)

    rim_2.wait()
    rim(2)

    def patch(i, j, tz):
        return fine[2 * i + tz - 1, 2 * j:2 * j + 3].reshape(576, 128)

    def middle_row(i, y, act):
        sig = jax.nn.sigmoid(act)
        if i < 2:
            hid[i, y] = (act * sig).astype(BF16)
        m = (i % 2 * 2 + y % 2) * 64
        back = (hidden_above if i == 2 else hidden_grad)[m:m + 64, (y // 2) * 128:(y // 2 + 1) * 128]
        pre_grad = (back * (sig * (1.0 + act * (1.0 - sig)))).astype(BF16)
        grad[i, y, 0:64, :] = pre_grad
        grad[i, y, 64:128, :] = pltpu.roll(pre_grad.astype(F32), 127, 1).astype(BF16)

    def inner_plane():
        taps = cat([cat([patch(1, j, tz) for j in range(4)], 1) for tz in range(3)], 0)
        pre_act = dot(w1_ref[...], taps, 1, 0)
        for y in range(4):
            middle_row(1, y, pre_act[:, y * 128:(y + 1) * 128])

    def face_plane(i, own, far):
        for y in range(4):
            at = slice(y * 64, (y + 1) * 64)
            middle_row(i, y, own[at] + far[at].astype(F32))

    def each(fn):
        def body(d, carry):
            fn(d)
            return carry

        lax.fori_loop(1, n, body, 0)

    def far_first(fn):
        def body(k, carry):
            down, up = n - k, k - 1
            down = jnp.where(down > me, down, down - 1)
            up = jnp.where(up < me, up, up + 1)
            fn(lax.rem(jnp.where(2 * me < n, down, up) + n - me, n))
            return carry

        lax.fori_loop(1, n, body, 0)

    sums, xbuf, chunks = (sums_0, sums_1), (xbuf_0, xbuf_1), (chunks_0, chunks_1)
    rs, ag, other = (rs_0, rs_1), (ag_0, ag_1), (other_0, other_1)

    def pair(k):
        return pltpu.make_async_remote_copy(
            src_ref=sums[k].at[1 - pen], dst_ref=xbuf[k], send_sem=pair_s.at[k], recv_sem=pair_r.at[k],
            device_id={"pencil": mate}, device_id_type=MESH)

    def rs_copy(k, d):
        to = lax.rem(me + d, n)
        return pltpu.make_async_remote_copy(
            src_ref=chunks[k].at[to], dst_ref=rs[k].at[d], send_sem=rs_s.at[k * n + d], recv_sem=rs_r.at[k * n + d],
            device_id={"slab": to}, device_id_type=MESH)

    def ag_copy(k, d, source):
        return pltpu.make_async_remote_copy(
            src_ref=ag[k].at[me], dst_ref=ag[k].at[source], send_sem=ag_s.at[k * n + d], recv_sem=ag_r.at[k * n + d],
            device_id={"slab": lax.rem(me + d, n)}, device_id_type=MESH)

    def forward(k, d):
        source = lax.rem(me + n - d, n)
        return pltpu.make_async_remote_copy(
            src_ref=ag[k].at[source], dst_ref=other[k].at[source], send_sem=fwd_s.at[k * n + d], recv_sem=fwd_r.at[k * n + d],
            device_id={"pencil": mate}, device_id_type=MESH)

    def begin(k):
        pair(k).wait_recv()
        total = sums[k][pen] + xbuf[k][...]
        for s in range(n):
            chunks[k][s] = total[s * rows:(s + 1) * rows].astype(RS_T)
        far_first(lambda d: rs_copy(k, d).start())

    def finish(k):
        each(lambda d: rs_copy(k, d).wait())
        mine = chunks[k][me].astype(F32)
        mine = lax.fori_loop(1, n, lambda d, acc: acc + rs[k][d].astype(F32), mine)
        ag[k][me] = mine.astype(AG_T)
        far_first(lambda d: ag_copy(k, d, me).start())
        forward(k, 0).start()

    def collect(k):
        def pass_on(d):
            ag_copy(k, d, lax.rem(me + n - d, n)).wait()
            forward(k, d).start()

        each(pass_on)
        forward(k, 0).wait()
        each(lambda d: forward(k, d).wait())

    def second_block(tz, ty):
        i, z = {1: (0, 0), 2: (0, 1), 0: (1, 1)}[tz]
        at = {1: ((0, 0), (1, 2)), 2: ((0, 1), (1, 3)), 0: ((1, 1), (2, 3))}[ty]
        left = cat([up[i, j] for j, y in at], 1)
        right = cat([hid[z, y] for j, y in at], 1)
        block = dot(left, right, 1, 1)
        return [block[tx * 64:(tx + 1) * 64] for tx in range(3)]

    def first_block(i, tz):
        cells = cat([grad[i, j, 0:64, :] for j in range(4)], 1)
        taps = cat([patch(i, j, tz) for j in range(4)], 1)
        return dot(cells, taps, 1, 1)

    inner_plane()
    taps_0 = [t for ty in range(3) for t in second_block(0, ty)]
    taps_2 = [t for ty in range(3) for t in second_block(2, ty)]
    sums_0[0] = cat(taps_0[:8], 1) * scales[1]
    sums_0[1] = cat(taps_2[:8], 1) * scales[1]
    pair(0).start()
    for tz in range(3):
        inner[tz] = first_block(1, tz)
    begin(0)
    part_up.wait()
    part_up0.wait()
    face_plane(0, down_own, up_in)
    part_down.wait()
    part_down0.wait()
    face_plane(2, up_own, down_in)
    low = pl.ds(0, 64)
    grad_y = send(grad.at[pl.ds(0, 3), 0, low], grad.at[pl.ds(0, 3), 4, low], 8, me, mate)

    taps_1 = [t for ty in range(3) for t in second_block(1, ty)]
    pad = jnp.zeros((64, 64), F32)
    sums_1[0, :, 512:896] = cat(taps_0[8:] + taps_1[:5], 1) * scales[1]
    sums_1[1, :, 512:896] = cat(taps_1[5:] + taps_2[8:] + [pad], 1) * scales[1]
    near = (inner[1] + first_block(0, 1)) * scales[0]
    last = (inner[2] + first_block(0, 2)) * scales[0]
    sums_1[0, :, 0:512] = near[:, 64:]
    sums_1[1, :, 0:512] = last[:, :512]
    base = (inner[0] + first_block(2, 0)) * scales[0]
    sums_1[0, :, 896:1280] = base[:, :384]
    sums_1[1, :, 896:1280] = cat([base[:, 384:], near[:, :64], last[:, 512:], pad], 1)
    pair(1).start()
    begin(1)
    pair(0).wait_send()
    pair(1).wait_send()

    grad_y.wait()
    for i, j in [(0, 4), (1, 4), (2, 4)]:
        here = grad[i, j, 0:64, :].astype(F32)
        grad[i, j, 64:128, :] = pltpu.roll(here, 127, 1).astype(BF16)

    def spread_plane(i):
        rhs = cat([cat([grad[i + a, j + b] for j in range(4)], 1) for a in range(2) for b in range(2)], 0)
        res = dot(wq[...], rhs, 0, 0)
        for pz in range(2):
            for py in range(2):
                for px in range(2):
                    m = ((pz * 2 + py) * 2 + px) * 64
                    for j in range(4):
                        at = pl.ds((2 * i + pz) * 8 + 2 * j + py, 64, stride=32)
                        xs[px, at, :] = res[m:m + 64, j * 128:(j + 1) * 128]

    join = select_matrix(256, 256, lambda r, c: c == jnp.where(r < 128, 2 * r, 2 * r - 255))

    spread_plane(0)
    spread_plane(1)
    finish(0)
    finish(1)
    both = cat([xs[0].astype(BF16), xs[1].astype(BF16)], 1)
    fg_ref[...] = dot(both, join, 1, 0).astype(BF16)

    places = (
        ((0, 0, 512, 1, 0), (1, 0, 512, 1, 1152)),
        ((0, 0, 512, 0, 640), (1, 0, 512, 0, 1152), (0, 512, 384, 1, 512), (1, 512, 256, 1, 896), (1, 768, 64, 1, 1664),
         (0, 896, 384, 0, 0), (1, 896, 256, 0, 384), (1, 1152, 64, 0, 1664)),
    )
    for k in range(2):
        collect(k)
        for owner, begins, size, g, to in places[k]:
            for s in range(n):
                own, far = ag[k][s, :, begins:begins + size].astype(F32), other[k][s, :, begins:begins + size].astype(F32)
                (g1_ref, g2_ref)[g][s * rows:(s + 1) * rows, to:to + size] = jnp.where(pen == owner, own, far)


def store(fg, g1, g2, fg_hbm, g1_hbm, g2_hbm, sem):
    pairs = ((fg, fg_hbm), (g1, g1_hbm), (g2, g2_hbm))
    copies = [pltpu.make_async_copy(a, b, sem.at[k]) for k, (a, b) in enumerate(pairs)]
    for copy in copies:
        copy.start()
    for copy in copies:
        copy.wait()


def local(fine_field, coarse_cotangent, first_weight, second_weight):
    n, npen = lax.axis_size("slab"), lax.axis_size("pencil")
    members = n * npen
    scales = (1.0 / math.sqrt(1024 * members), 1.0 / math.sqrt(128 * members))
    rows = 64 // n
    widths = (512, 1280)
    vmem = pl.BlockSpec(memory_space=pltpu.VMEM)
    hbm = pl.BlockSpec(memory_space=pltpu.HBM)
    dma = pltpu.SemaphoreType.DMA
    outs = (
        jax.ShapeDtypeStruct((2048, 256), BF16),
        jax.ShapeDtypeStruct((64, 1728), F32),
        jax.ShapeDtypeStruct((64, 1728), F32),
    )
    held = (pltpu.VMEM((2048, 256), BF16), pltpu.VMEM((64, 1728), F32), pltpu.VMEM((64, 1728), F32))
    operands = (fine_field.reshape(2048, 256), coarse_cotangent.reshape(128, 64), first_weight, second_weight)
    results = pl.pallas_call(
        functools.partial(kernel, n, npen, scales),
        out_shape=held,
        in_specs=[hbm] * 4,
        out_specs=(vmem, vmem, vmem),
        scratch_shapes=[
            pltpu.VMEM((2048, 256), BF16),
            pltpu.VMEM((128, 64), BF16),
            pltpu.VMEM((64, 1728), BF16),
            pltpu.VMEM((64, 1728), BF16),
            dma((4,)),
            pltpu.VMEM((2, 2048, 128), F32),
            pltpu.VMEM((4, 9, 192, 128), BF16),
            *[pltpu.VMEM((256, 128), BF16), pltpu.VMEM((256, 128), BF16), pltpu.VMEM((256, 128), F32)] * 2,
            pltpu.VMEM((3, 64, 576), F32),
            pltpu.VMEM((2, 3, 192, 128), BF16),
            pltpu.VMEM((3, 5, 128, 128), BF16),
            pltpu.VMEM((2, 4, 64, 128), BF16),
            pltpu.VMEM((128, 128), F32),
            pltpu.VMEM((512, 512), BF16),
            pltpu.VMEM((768, 256), BF16),
            *[pltpu.VMEM((2, 64, w), F32) for w in widths],
            *[pltpu.VMEM((64, w), F32) for w in widths],
            *[pltpu.VMEM((n, rows, w), RS_T) for w in widths],
            *[pltpu.VMEM((n, rows, w), RS_T) for w in widths],
            *[pltpu.VMEM((n, rows, w), AG_T) for w in widths],
            *[pltpu.VMEM((n, rows, w), AG_T) for w in widths],
            dma((11,)), dma((11,)), dma((2 * n,)), dma((2 * n,)), dma((2 * n,)), dma((2 * n,)), dma((2,)), dma((2,)), dma((2 * n,)), dma((2 * n,)),
        ],
        compiler_params=pltpu.CompilerParams(
            collective_id=0, has_side_effects=True, vmem_limit_bytes=40 * 1024 * 1024),
    )(*[pltpu.with_memory_space_constraint(v, pltpu.HBM) for v in operands])
    results = [pltpu.with_memory_space_constraint(v, pltpu.VMEM) for v in results]
    fine_grad, first_grad, second_grad = pl.pallas_call(
        store,
        out_shape=outs,
        in_specs=[vmem] * 3,
        out_specs=(hbm,) * 3,
        scratch_shapes=[dma((3,))],
    )(*results)
    return fine_grad.reshape(fine_field.shape), first_grad, second_grad


def solution(mesh):
    placed = (P("groups", "slab", "pencil", None), P("groups", "slab", "pencil", None), P(), P())
    return jax.shard_map(
        local,
        mesh=mesh,
        in_specs=placed,
        out_specs=(P("groups", "slab", "pencil", None), P("groups", None), P("groups", None)),
        check_vma=False,
    )
```

```python
import functools
import math

import jax
import jax.numpy as jnp
from jax import lax
from jax.experimental import pallas as pl
from jax.experimental.pallas import tpu as pltpu
from jax.sharding import PartitionSpec as P

MESH = pl.DeviceIdType.MESH
F32, BF16 = jnp.float32, jnp.bfloat16
RS_T, AG_T = BF16, BF16
TAP = {(0, 0): 1, (1, 0): 2, (1, 1): 0}


def tap(parity, off):
    return TAP.get((parity, off))


def dot(a, b, da, db):
    return lax.dot_general(a, b, (((da,), (db,)), ((), ())), preferred_element_type=F32)


def cat(parts, axis):
    return jnp.concatenate(parts, axis=axis)


def select_matrix(rows, columns, fn):
    row = lax.broadcasted_iota(jnp.int32, (rows, columns), 0)
    col = lax.broadcasted_iota(jnp.int32, (rows, columns), 1)
    return jnp.where(fn(row, col), 1.0, 0.0).astype(BF16)


def kernel(n, npen, scales, x_hbm, cot_hbm, w1_hbm, w2_hbm, fg_ref, g1_ref, g2_ref,
           x_ref, cot_ref, w1_ref, w2_ref, in_sem, xs, fine, up_out, up_in, up_own, down_out, down_in, down_own, inner, up, grad, hid, cs, wq, w2q, sums_0, sums_1, xbuf_0, xbuf_1, chunks_0, chunks_1, rs_0, rs_1, ag_0, ag_1, other_0, other_1,
           halo_s, halo_r, rs_s, rs_r, ag_s, ag_r, pair_s, pair_r, fwd_s, fwd_r):
    me = lax.axis_index("slab")
    pen = lax.axis_index("pencil")
    above = lax.rem(me + 1, n)
    below = lax.rem(me + n - 1, n)
    mate = lax.rem(pen + 1, npen)
    rows = 64 // n

    barrier = pltpu.get_barrier_semaphore()

    def greet(s, p):
        pl.semaphore_signal(barrier, inc=1, device_id={"slab": s, "pencil": p}, device_id_type=MESH)

    def greet_peer(d, carry):
        greet(lax.rem(me + d, n), pen)
        return carry

    cot_in = pltpu.make_async_copy(cot_hbm, cot_ref, in_sem.at[0])
    cot_in.start()
    x_in = pltpu.make_async_copy(x_hbm, x_ref, in_sem.at[3])
    x_in.start()
    w1_in = pltpu.make_async_copy(w1_hbm, w1_ref, in_sem.at[1])
    w1_in.start()
    w2_in = pltpu.make_async_copy(w2_hbm, w2_ref, in_sem.at[2])
    w2_in.start()

    lax.fori_loop(1, n, greet_peer, 0)
    greet(me, mate)
    greet(above, mate)
    greet(below, mate)

    def send(src, dst, k, s, p):
        copy = pltpu.make_async_remote_copy(
            src_ref=src, dst_ref=dst, send_sem=halo_s.at[k], recv_sem=halo_r.at[k],
            device_id={"slab": s, "pencil": p}, device_id_type=MESH)
        copy.start()
        return copy

    spread = select_matrix(64, 128, lambda r, c: c == 2 * r)
    cot_in.wait()
    cs[...] = dot(cot_ref[...], spread, 1, 0)
    for j in range(2):
        up[0, j, 64:128, :] = cs[pl.ds(j, 64, stride=2), :].astype(BF16)

    pl.semaphore_wait(barrier, n + 2)
    halves = pl.ds(64, 128)
    middle = pl.ds(64, 64)
    up_z = send(up.at[0, pl.ds(0, 2), middle], up.at[1, pl.ds(0, 2), middle], 0, below, pen)
    up_y = send(up.at[0, 0, middle], up.at[0, 2, middle], 1, me, mate)
    up_c = send(up.at[0, 0, middle], up.at[1, 2, middle], 2, below, mate)

    split = select_matrix(256, 256, lambda r, c: r == jnp.where(c < 128, 2 * c, 2 * c - 255))

    x_in.wait()
    both = dot(x_ref[...], split, 1, 0)
    xs[0] = both[:, :128]
    xs[1] = both[:, 128:]

    def plane(z, y):
        at = pl.ds(z * 8 + y, 64, stride=32)
        even, odd = xs[0, at, :], xs[1, at, :]
        fine[z, y + 1, 64:128, :] = even.astype(BF16)
        fine[z, y + 1, 128:192, :] = odd.astype(BF16)
        fine[z, y + 1, 0:64, :] = pltpu.roll(odd, 1, 1).astype(BF16)

    def rim_send(z, count, k):
        at = pl.ds(z, count)
        return send(fine.at[at, 8, halves], fine.at[at, 0, halves], k, me, mate)

    def rim(z):
        odd = fine[z, 0, 128:192, :].astype(F32)
        fine[z, 0, 0:64, :] = pltpu.roll(odd, 1, 1).astype(BF16)

    def column(z, j):
        return fine[z, 2 * j:2 * j + 3].reshape(576, 128)

    def partial_sum(own, out, landing, k, to, planes, weight, first):
        at = slice(0, 1) if first else slice(1, 4)
        taps = cat([cat([column(z, j) for j in range(4)[at]], 1) for z in planes], 0)
        res = dot(weight, taps, 1, 0)
        piece = pl.ds(0, 64) if first else pl.ds(64, 192)
        for j in range(4)[at]:
            c = res[:, (j - at.start) * 128:(j - at.start + 1) * 128]
            own[j * 64:(j + 1) * 64] = c
            out[j * 64:(j + 1) * 64] = c.astype(BF16)
        return send(out.at[piece], landing.at[piece], k, to, pen)

    plane(3, 7)
    rim_3 = rim_send(3, 1, 3)
    for y in range(7):
        plane(3, y)
    w1_in.wait()
    part_up = partial_sum(up_own, up_out, up_in, 4, above, (3,), w1_ref[:, 0:576], False)
    plane(0, 7)
    plane(1, 7)
    rim_01 = rim_send(0, 2, 5)
    for z in range(2):
        for y in range(7):
            plane(z, y)
    part_down = partial_sum(down_own, down_out, down_in, 6, below, (0, 1), w1_ref[:, 576:], False)
    plane(2, 7)
    rim_2 = rim_send(2, 1, 7)
    rim_3.wait()
    rim(3)
    part_up0 = partial_sum(up_own, up_out, up_in, 9, above, (3,), w1_ref[:, 0:576], True)
    rim_01.wait()
    rim(0)
    rim(1)
    part_down0 = partial_sum(down_own, down_out, down_in, 10, below, (0, 1), w1_ref[:, 576:], True)
    for y in range(7):
        plane(2, y)

    w2_in.wait()
    wq[...] = jnp.zeros_like(wq)
    w2q[...] = jnp.zeros_like(w2q)
    for a in range(2):
        for b in range(2):
            for pz in range(2):
                for py in range(2):
                    tz, ty = tap(pz, a), tap(py, b)
                    if tz is None or ty is None:
                        continue
                    for tx in range(3):
                        t = ((tz * 3 + ty) * 3 + tx) * 64
                        px, r = {1: (0, 0), 2: (1, 0), 0: (1, 1)}[tx]
                        k = ((a * 2 + b) * 2 + r) * 64
                        m = ((pz * 2 + py) * 2 + px) * 64
                        wq[k:k + 64, m:m + 64] = w1_ref[:, t:t + 64]
                        k2 = ((a * 2 + b) * 3 + tx) * 64
                        m2 = (pz * 2 + py) * 64
                        w2q[k2:k2 + 64, m2:m2 + 64] = w2_ref[:, t:t + 64]

    up_z.wait()
    up_y.wait()
    up_c.wait()
    for i in range(2):
        for j in range(3):
            mid = up[i, j, 64:128, :].astype(F32)
            up[i, j, 0:64, :] = pltpu.roll(mid, 127, 1).astype(BF16)
            up[i, j, 128:192, :] = pltpu.roll(mid, 1, 1).astype(BF16)
    rhs = cat([cat([up[a, j + b] for j in range(2)], 1) for a in range(2) for b in range(2)], 0)
    hidden_grad = dot(w2q[...], rhs, 0, 0)
    rhs = cat([cat([up[1, j + b] for j in range(2)], 1) for b in range(2)], 0)
    hidden_above = dot(w2q[0:384, 0:128], rhs, 0, 0)

    rim_2.wait()
    rim(2)

    def patch(i, j, tz):
        return fine[2 * i + tz - 1, 2 * j:2 * j + 3].reshape(576, 128)

    def middle_row(i, y, act):
        sig = jax.nn.sigmoid(act)
        if i < 2:
            hid[i, y] = (act * sig).astype(BF16)
        m = (i % 2 * 2 + y % 2) * 64
        back = (hidden_above if i == 2 else hidden_grad)[m:m + 64, (y // 2) * 128:(y // 2 + 1) * 128]
        pre_grad = (back * (sig * (1.0 + act * (1.0 - sig)))).astype(BF16)
        grad[i, y, 0:64, :] = pre_grad
        grad[i, y, 64:128, :] = pltpu.roll(pre_grad.astype(F32), 127, 1).astype(BF16)

    def inner_plane():
        taps = cat([cat([patch(1, j, tz) for j in range(4)], 1) for tz in range(3)], 0)
        pre_act = dot(w1_ref[...], taps, 1, 0)
        for y in range(4):
            middle_row(1, y, pre_act[:, y * 128:(y + 1) * 128])

    def face_plane(i, own, far):
        for y in range(4):
            at = slice(y * 64, (y + 1) * 64)
            middle_row(i, y, own[at] + far[at].astype(F32))

    def each(fn):
        def body(d, carry):
            fn(d)
            return carry

        lax.fori_loop(1, n, body, 0)

    def far_first(fn):
        def body(k, carry):
            down, up = n - k, k - 1
            down = jnp.where(down > me, down, down - 1)
            up = jnp.where(up < me, up, up + 1)
            fn(lax.rem(jnp.where(2 * me < n, down, up) + n - me, n))
            return carry

        lax.fori_loop(1, n, body, 0)

    sums, xbuf, chunks = (sums_0, sums_1), (xbuf_0, xbuf_1), (chunks_0, chunks_1)
    rs, ag, other = (rs_0, rs_1), (ag_0, ag_1), (other_0, other_1)

    pieces = ((0, 0, 512), (1, 0, 896), (1, 896, 384))

    def pair(p):
        k, begins, size = pieces[p]
        at = pl.ds(begins, size)
        return pltpu.make_async_remote_copy(
            src_ref=sums[k].at[1 - pen, :, at], dst_ref=xbuf[k].at[:, at], send_sem=pair_s.at[p], recv_sem=pair_r.at[p],
            device_id={"pencil": mate}, device_id_type=MESH)

    def rs_copy(k, d):
        to = lax.rem(me + d, n)
        return pltpu.make_async_remote_copy(
            src_ref=chunks[k].at[to], dst_ref=rs[k].at[d], send_sem=rs_s.at[k * n + d], recv_sem=rs_r.at[k * n + d],
            device_id={"slab": to}, device_id_type=MESH)

    def ag_copy(k, d, source):
        return pltpu.make_async_remote_copy(
            src_ref=ag[k].at[me], dst_ref=ag[k].at[source], send_sem=ag_s.at[k * n + d], recv_sem=ag_r.at[k * n + d],
            device_id={"slab": lax.rem(me + d, n)}, device_id_type=MESH)

    def forward(k, d):
        source = lax.rem(me + n - d, n)
        return pltpu.make_async_remote_copy(
            src_ref=ag[k].at[source], dst_ref=other[k].at[source], send_sem=fwd_s.at[k * n + d], recv_sem=fwd_r.at[k * n + d],
            device_id={"pencil": mate}, device_id_type=MESH)

    partner = me + 1 - 2 * lax.rem(me, 2)

    def stride_copy(d, source):
        return pltpu.make_async_remote_copy(
            src_ref=ag[0].at[me], dst_ref=ag[0].at[source], send_sem=ag_s.at[d], recv_sem=ag_r.at[d],
            device_id={"slab": lax.rem(me + 2 * d, n)}, device_id_type=MESH)

    def relay_copy(d, landing):
        return pltpu.make_async_remote_copy(
            src_ref=ag[0].at[lax.rem(me + n - 2 * d, n)], dst_ref=ag[0].at[landing], send_sem=ag_s.at[n // 2 + d], recv_sem=ag_r.at[n // 2 + d],
            device_id={"slab": partner}, device_id_type=MESH)

    def relay(d, carry):
        source = lax.rem(me + n - 2 * d, n)
        stride_copy(d, source).wait()
        relay_copy(d, source).start()
        return carry

    def relayed(d, carry):
        relay_copy(d, lax.rem(partner + n - 2 * d, n)).wait()
        return carry

    def begin(k):
        for p in range(3):
            if pieces[p][0] == k:
                pair(p).wait_recv()
        total = sums[k][pen] + xbuf[k][...]
        for s in range(n):
            chunks[k][s] = total[s * rows:(s + 1) * rows].astype(RS_T)
        far_first(lambda d: rs_copy(k, d).start())

    def finish(k):
        each(lambda d: rs_copy(k, d).wait())
        mine = chunks[k][me].astype(F32)
        mine = lax.fori_loop(1, n, lambda d, acc: acc + rs[k][d].astype(F32), mine)
        ag[k][me] = mine.astype(AG_T)
        if k == 0:
            lax.fori_loop(1, n // 2, lambda d, c: stride_copy(d, me).start() or c, 0)
            relay_copy(0, me).start()
        else:
            far_first(lambda d: ag_copy(k, d, me).start())
        if k > 0:
            forward(k, 0).start()

    def collect(k):
        if k == 0:
            lax.fori_loop(1, n // 2, relay, 0)
            lax.fori_loop(0, n // 2, relayed, 0)
            whole = pltpu.make_async_remote_copy(
                src_ref=ag[k], dst_ref=other[k], send_sem=fwd_s.at[0], recv_sem=fwd_r.at[0],
                device_id={"pencil": mate}, device_id_type=MESH)
            whole.start()
            return whole
        forward(k, 0).wait()
        each(lambda d: forward(k, d).wait())

    def pass_on(k, d):
        ag_copy(k, d, lax.rem(me + n - d, n)).wait()
        forward(k, d).start()

    def second_block(tz, ty):
        i, z = {1: (0, 0), 2: (0, 1), 0: (1, 1)}[tz]
        at = {1: ((0, 0), (1, 2)), 2: ((0, 1), (1, 3)), 0: ((1, 1), (2, 3))}[ty]
        left = cat([up[i, j] for j, y in at], 1)
        right = cat([hid[z, y] for j, y in at], 1)
        block = dot(left, right, 1, 1)
        return [block[tx * 64:(tx + 1) * 64] for tx in range(3)]

    def first_block(i, tz):
        cells = cat([grad[i, j, 0:64, :] for j in range(4)], 1)
        taps = cat([patch(i, j, tz) for j in range(4)], 1)
        return dot(cells, taps, 1, 1)

    inner_plane()
    taps_0 = [t for ty in range(3) for t in second_block(0, ty)]
    taps_2 = [t for ty in range(3) for t in second_block(2, ty)]
    sums_0[0] = cat(taps_0[:8], 1) * scales[1]
    sums_0[1] = cat(taps_2[:8], 1) * scales[1]
    pair(0).start()
    for tz in range(3):
        inner[tz] = first_block(1, tz)
    part_up.wait()
    part_up0.wait()
    face_plane(0, down_own, up_in)
    begin(0)
    part_down.wait()
    part_down0.wait()
    face_plane(2, up_own, down_in)
    low = pl.ds(0, 64)
    grad_y = send(grad.at[pl.ds(0, 3), 0, low], grad.at[pl.ds(0, 3), 4, low], 8, me, mate)

    taps_1 = [t for ty in range(3) for t in second_block(1, ty)]
    pad = jnp.zeros((64, 64), F32)
    sums_1[0, :, 512:896] = cat(taps_0[8:] + taps_1[:5], 1) * scales[1]
    sums_1[1, :, 512:896] = cat(taps_1[5:] + taps_2[8:] + [pad], 1) * scales[1]
    near = (inner[1] + first_block(0, 1)) * scales[0]
    last = (inner[2] + first_block(0, 2)) * scales[0]
    sums_1[0, :, 0:512] = near[:, 64:]
    sums_1[1, :, 0:512] = last[:, :512]
    pair(1).start()
    base = (inner[0] + first_block(2, 0)) * scales[0]
    sums_1[0, :, 896:1280] = base[:, :384]
    sums_1[1, :, 896:1280] = cat([base[:, 384:], near[:, :64], last[:, 512:], pad], 1)
    pair(2).start()
    begin(1)
    pair(0).wait_send()
    pair(1).wait_send()
    pair(2).wait_send()

    grad_y.wait()
    for i, j in [(0, 4), (1, 4), (2, 4)]:
        here = grad[i, j, 0:64, :].astype(F32)
        grad[i, j, 64:128, :] = pltpu.roll(here, 127, 1).astype(BF16)

    def spread_plane(i):
        rhs = cat([cat([grad[i + a, j + b] for j in range(4)], 1) for a in range(2) for b in range(2)], 0)
        res = dot(wq[...], rhs, 0, 0)
        for pz in range(2):
            for py in range(2):
                for px in range(2):
                    m = ((pz * 2 + py) * 2 + px) * 64
                    for j in range(4):
                        at = pl.ds((2 * i + pz) * 8 + 2 * j + py, 64, stride=32)
                        xs[px, at, :] = res[m:m + 64, j * 128:(j + 1) * 128]

    join = select_matrix(256, 256, lambda r, c: c == jnp.where(r < 128, 2 * r, 2 * r - 255))

    spread_plane(0)
    spread_plane(1)
    finish(0)
    both = cat([xs[0].astype(BF16), xs[1].astype(BF16)], 1)
    fg_ref[...] = dot(both, join, 1, 0).astype(BF16)

    finish(1)
    places = (
        ((0, 0, 512, 1, 0), (1, 0, 512, 1, 1152)),
        ((0, 0, 512, 0, 640), (1, 0, 512, 0, 1152), (0, 512, 384, 1, 512), (1, 512, 256, 1, 896), (1, 768, 64, 1, 1664),
         (0, 896, 384, 0, 0), (1, 896, 256, 0, 384), (1, 1152, 64, 0, 1664)),
    )
    whole = collect(0)
    each(lambda d: pass_on(1, d))
    for k in range(2):
        whole.wait() if k == 0 else collect(1)
        for owner, begins, size, g, to in places[k]:
            for s in range(n):
                own, far = ag[k][s, :, begins:begins + size].astype(F32), other[k][s, :, begins:begins + size].astype(F32)
                (g1_ref, g2_ref)[g][s * rows:(s + 1) * rows, to:to + size] = jnp.where(pen == owner, own, far)


def store(fg, g1, g2, fg_hbm, g1_hbm, g2_hbm, sem):
    pairs = ((fg, fg_hbm), (g1, g1_hbm), (g2, g2_hbm))
    copies = [pltpu.make_async_copy(a, b, sem.at[k]) for k, (a, b) in enumerate(pairs)]
    for copy in copies:
        copy.start()
    for copy in copies:
        copy.wait()


def local(fine_field, coarse_cotangent, first_weight, second_weight):
    n, npen = lax.axis_size("slab"), lax.axis_size("pencil")
    members = n * npen
    scales = (1.0 / math.sqrt(1024 * members), 1.0 / math.sqrt(128 * members))
    rows = 64 // n
    widths = (512, 1280)
    vmem = pl.BlockSpec(memory_space=pltpu.VMEM)
    hbm = pl.BlockSpec(memory_space=pltpu.HBM)
    dma = pltpu.SemaphoreType.DMA
    outs = (
        jax.ShapeDtypeStruct((2048, 256), BF16),
        jax.ShapeDtypeStruct((64, 1728), F32),
        jax.ShapeDtypeStruct((64, 1728), F32),
    )
    held = (pltpu.VMEM((2048, 256), BF16), pltpu.VMEM((64, 1728), F32), pltpu.VMEM((64, 1728), F32))
    operands = (fine_field.reshape(2048, 256), coarse_cotangent.reshape(128, 64), first_weight, second_weight)
    results = pl.pallas_call(
        functools.partial(kernel, n, npen, scales),
        out_shape=held,
        in_specs=[hbm] * 4,
        out_specs=(vmem, vmem, vmem),
        scratch_shapes=[
            pltpu.VMEM((2048, 256), BF16),
            pltpu.VMEM((128, 64), BF16),
            pltpu.VMEM((64, 1728), BF16),
            pltpu.VMEM((64, 1728), BF16),
            dma((4,)),
            pltpu.VMEM((2, 2048, 128), F32),
            pltpu.VMEM((4, 9, 192, 128), BF16),
            *[pltpu.VMEM((256, 128), BF16), pltpu.VMEM((256, 128), BF16), pltpu.VMEM((256, 128), F32)] * 2,
            pltpu.VMEM((3, 64, 576), F32),
            pltpu.VMEM((2, 3, 192, 128), BF16),
            pltpu.VMEM((3, 5, 128, 128), BF16),
            pltpu.VMEM((2, 4, 64, 128), BF16),
            pltpu.VMEM((128, 128), F32),
            pltpu.VMEM((512, 512), BF16),
            pltpu.VMEM((768, 256), BF16),
            *[pltpu.VMEM((2, 64, w), F32) for w in widths],
            *[pltpu.VMEM((64, w), F32) for w in widths],
            *[pltpu.VMEM((n, rows, w), RS_T) for w in widths],
            *[pltpu.VMEM((n, rows, w), RS_T) for w in widths],
            *[pltpu.VMEM((n, rows, w), AG_T) for w in widths],
            *[pltpu.VMEM((n, rows, w), AG_T) for w in widths],
            dma((11,)), dma((11,)), dma((2 * n,)), dma((2 * n,)), dma((2 * n,)), dma((2 * n,)), dma((3,)), dma((3,)), dma((2 * n,)), dma((2 * n,)),
        ],
        compiler_params=pltpu.CompilerParams(
            collective_id=0, has_side_effects=True, vmem_limit_bytes=40 * 1024 * 1024),
    )(*[pltpu.with_memory_space_constraint(v, pltpu.HBM) for v in operands])
    results = [pltpu.with_memory_space_constraint(v, pltpu.VMEM) for v in results]
    fine_grad, first_grad, second_grad = pl.pallas_call(
        store,
        out_shape=outs,
        in_specs=[vmem] * 3,
        out_specs=(hbm,) * 3,
        scratch_shapes=[dma((3,))],
    )(*results)
    return fine_grad.reshape(fine_field.shape), first_grad, second_grad


def solution(mesh):
    placed = (P("groups", "slab", "pencil", None), P("groups", "slab", "pencil", None), P(), P())
    return jax.shard_map(
        local,
        mesh=mesh,
        in_specs=placed,
        out_specs=(P("groups", "slab", "pencil", None), P("groups", None), P("groups", None)),
        check_vma=False,
    )
```

```python
import functools
import math

import jax
import jax.numpy as jnp
from jax import lax
from jax.experimental import pallas as pl
from jax.experimental.pallas import tpu as pltpu
from jax.sharding import PartitionSpec as P

MESH = pl.DeviceIdType.MESH
F32, BF16 = jnp.float32, jnp.bfloat16
RS_T, AG_T = BF16, BF16
TAP = {(0, 0): 1, (1, 0): 2, (1, 1): 0}


def tap(parity, off):
    return TAP.get((parity, off))


def dot(a, b, da, db):
    return lax.dot_general(a, b, (((da,), (db,)), ((), ())), preferred_element_type=F32)


def cat(parts, axis):
    return jnp.concatenate(parts, axis=axis)


def select_matrix(rows, columns, fn):
    row = lax.broadcasted_iota(jnp.int32, (rows, columns), 0)
    col = lax.broadcasted_iota(jnp.int32, (rows, columns), 1)
    return jnp.where(fn(row, col), 1.0, 0.0).astype(BF16)


def kernel(n, npen, scales, x_hbm, cot_hbm, w1_hbm, w2_hbm, fg_ref, g1_ref, g2_ref,
           x_ref, cot_ref, w1_ref, w2_ref, in_sem, xs, fine, up_out, up_in, up_own, down_out, down_in, down_own, inner, up, grad, hid, cs, wq, w2q, sums_0, sums_1, xbuf_0, xbuf_1, chunks_0, chunks_1, rs_0, rs_1, ag_0, ag_1, other_0, other_1,
           halo_s, halo_r, rs_s, rs_r, ag_s, ag_r, pair_s, pair_r, fwd_s, fwd_r):
    me = lax.axis_index("slab")
    pen = lax.axis_index("pencil")
    above = lax.rem(me + 1, n)
    below = lax.rem(me + n - 1, n)
    mate = lax.rem(pen + 1, npen)
    rows = 64 // n

    barrier = pltpu.get_barrier_semaphore()

    def greet(s, p):
        pl.semaphore_signal(barrier, inc=1, device_id={"slab": s, "pencil": p}, device_id_type=MESH)

    def greet_peer(d, carry):
        greet(lax.rem(me + d, n), pen)
        return carry

    cot_in = pltpu.make_async_copy(cot_hbm, cot_ref, in_sem.at[0])
    cot_in.start()
    x_in = pltpu.make_async_copy(x_hbm, x_ref, in_sem.at[3])
    x_in.start()
    w1_in = pltpu.make_async_copy(w1_hbm, w1_ref, in_sem.at[1])
    w1_in.start()
    w2_in = pltpu.make_async_copy(w2_hbm, w2_ref, in_sem.at[2])
    w2_in.start()

    lax.fori_loop(1, n, greet_peer, 0)
    greet(me, mate)
    greet(above, mate)
    greet(below, mate)

    def send(src, dst, k, s, p):
        copy = pltpu.make_async_remote_copy(
            src_ref=src, dst_ref=dst, send_sem=halo_s.at[k], recv_sem=halo_r.at[k],
            device_id={"slab": s, "pencil": p}, device_id_type=MESH)
        copy.start()
        return copy

    spread = select_matrix(64, 128, lambda r, c: c == 2 * r)
    cot_in.wait()
    cs[...] = dot(cot_ref[...], spread, 1, 0)
    for j in range(2):
        up[0, j, 64:128, :] = cs[pl.ds(j, 64, stride=2), :].astype(BF16)

    split = select_matrix(256, 256, lambda r, c: r == jnp.where(c < 128, 2 * c, 2 * c - 255))

    x_in.wait()
    both = dot(x_ref[...], split, 1, 0)
    xs[0] = both[:, :128]
    xs[1] = both[:, 128:]

    pl.semaphore_wait(barrier, n + 2)
    halves = pl.ds(64, 128)
    middle = pl.ds(64, 64)
    up_z = send(up.at[0, pl.ds(0, 2), middle], up.at[1, pl.ds(0, 2), middle], 0, below, pen)
    up_y = send(up.at[0, 0, middle], up.at[0, 2, middle], 1, me, mate)
    up_c = send(up.at[0, 0, middle], up.at[1, 2, middle], 2, below, mate)

    def plane(z, y):
        at = pl.ds(z * 8 + y, 64, stride=32)
        even, odd = xs[0, at, :], xs[1, at, :]
        fine[z, y + 1, 64:128, :] = even.astype(BF16)
        fine[z, y + 1, 128:192, :] = odd.astype(BF16)
        fine[z, y + 1, 0:64, :] = pltpu.roll(odd, 1, 1).astype(BF16)

    def rim_send(z, count, k):
        at = pl.ds(z, count)
        return send(fine.at[at, 8, halves], fine.at[at, 0, halves], k, me, mate)

    def rim(z):
        odd = fine[z, 0, 128:192, :].astype(F32)
        fine[z, 0, 0:64, :] = pltpu.roll(odd, 1, 1).astype(BF16)

    def column(z, j):
        return fine[z, 2 * j:2 * j + 3].reshape(576, 128)

    def partial_sum(own, out, landing, k, to, planes, weight, first):
        at = slice(0, 1) if first else slice(1, 4)
        taps = cat([cat([column(z, j) for j in range(4)[at]], 1) for z in planes], 0)
        res = dot(weight, taps, 1, 0)
        piece = pl.ds(0, 64) if first else pl.ds(64, 192)
        for j in range(4)[at]:
            c = res[:, (j - at.start) * 128:(j - at.start + 1) * 128]
            own[j * 64:(j + 1) * 64] = c
            out[j * 64:(j + 1) * 64] = c.astype(BF16)
        return send(out.at[piece], landing.at[piece], k, to, pen)

    plane(3, 7)
    rim_3 = rim_send(3, 1, 3)
    for y in range(7):
        plane(3, y)
    w1_in.wait()
    part_up = partial_sum(up_own, up_out, up_in, 4, above, (3,), w1_ref[:, 0:576], False)
    plane(0, 7)
    plane(1, 7)
    rim_01 = rim_send(0, 2, 5)
    for z in range(2):
        for y in range(7):
            plane(z, y)
    part_down = partial_sum(down_own, down_out, down_in, 6, below, (0, 1), w1_ref[:, 576:], False)
    plane(2, 7)
    rim_2 = rim_send(2, 1, 7)
    rim_3.wait()
    rim(3)
    part_up0 = partial_sum(up_own, up_out, up_in, 9, above, (3,), w1_ref[:, 0:576], True)
    rim_01.wait()
    rim(0)
    rim(1)
    part_down0 = partial_sum(down_own, down_out, down_in, 10, below, (0, 1), w1_ref[:, 576:], True)
    for y in range(7):
        plane(2, y)

    w2_in.wait()
    wq[...] = jnp.zeros_like(wq)
    w2q[...] = jnp.zeros_like(w2q)
    for a in range(2):
        for b in range(2):
            for pz in range(2):
                for py in range(2):
                    tz, ty = tap(pz, a), tap(py, b)
                    if tz is None or ty is None:
                        continue
                    for tx in range(3):
                        t = ((tz * 3 + ty) * 3 + tx) * 64
                        px, r = {1: (0, 0), 2: (1, 0), 0: (1, 1)}[tx]
                        k = ((a * 2 + b) * 2 + r) * 64
                        m = ((pz * 2 + py) * 2 + px) * 64
                        wq[k:k + 64, m:m + 64] = w1_ref[:, t:t + 64]
                        k2 = ((a * 2 + b) * 3 + tx) * 64
                        m2 = (pz * 2 + py) * 64
                        w2q[k2:k2 + 64, m2:m2 + 64] = w2_ref[:, t:t + 64]

    up_z.wait()
    up_y.wait()
    up_c.wait()
    for i in range(2):
        for j in range(3):
            mid = up[i, j, 64:128, :].astype(F32)
            up[i, j, 0:64, :] = pltpu.roll(mid, 127, 1).astype(BF16)
            up[i, j, 128:192, :] = pltpu.roll(mid, 1, 1).astype(BF16)
    rhs = cat([cat([up[a, j + b] for j in range(2)], 1) for a in range(2) for b in range(2)], 0)
    hidden_grad = dot(w2q[...], rhs, 0, 0)
    rhs = cat([cat([up[1, j + b] for j in range(2)], 1) for b in range(2)], 0)
    hidden_above = dot(w2q[0:384, 0:128], rhs, 0, 0)

    rim_2.wait()
    rim(2)

    def patch(i, j, tz):
        return fine[2 * i + tz - 1, 2 * j:2 * j + 3].reshape(576, 128)

    def middle_row(i, y, act):
        sig = jax.nn.sigmoid(act)
        if i < 2:
            hid[i, y] = (act * sig).astype(BF16)
        m = (i % 2 * 2 + y % 2) * 64
        back = (hidden_above if i == 2 else hidden_grad)[m:m + 64, (y // 2) * 128:(y // 2 + 1) * 128]
        pre_grad = (back * (sig * (1.0 + act * (1.0 - sig)))).astype(BF16)
        grad[i, y, 0:64, :] = pre_grad
        grad[i, y, 64:128, :] = pltpu.roll(pre_grad.astype(F32), 127, 1).astype(BF16)

    def inner_plane():
        taps = cat([cat([patch(1, j, tz) for j in range(4)], 1) for tz in range(3)], 0)
        pre_act = dot(w1_ref[...], taps, 1, 0)
        for y in range(4):
            middle_row(1, y, pre_act[:, y * 128:(y + 1) * 128])

    def face_plane(i, own, far):
        for y in range(4):
            at = slice(y * 64, (y + 1) * 64)
            middle_row(i, y, own[at] + far[at].astype(F32))

    def each(fn):
        def body(d, carry):
            fn(d)
            return carry

        lax.fori_loop(1, n, body, 0)

    def far_first(fn):
        def body(k, carry):
            down, up = n - k, k - 1
            down = jnp.where(down > me, down, down - 1)
            up = jnp.where(up < me, up, up + 1)
            fn(lax.rem(jnp.where(2 * me < n, down, up) + n - me, n))
            return carry

        lax.fori_loop(1, n, body, 0)

    sums, xbuf, chunks = (sums_0, sums_1), (xbuf_0, xbuf_1), (chunks_0, chunks_1)
    rs, ag, other = (rs_0, rs_1), (ag_0, ag_1), (other_0, other_1)

    pieces = ((0, 0, 512), (1, 0, 896), (1, 896, 384))

    def pair(p):
        k, begins, size = pieces[p]
        at = pl.ds(begins, size)
        return pltpu.make_async_remote_copy(
            src_ref=sums[k].at[1 - pen, :, at], dst_ref=xbuf[k].at[:, at], send_sem=pair_s.at[p], recv_sem=pair_r.at[p],
            device_id={"pencil": mate}, device_id_type=MESH)

    def rs_copy(k, d):
        to = lax.rem(me + d, n)
        return pltpu.make_async_remote_copy(
            src_ref=chunks[k].at[to], dst_ref=rs[k].at[d], send_sem=rs_s.at[k * n + d], recv_sem=rs_r.at[k * n + d],
            device_id={"slab": to}, device_id_type=MESH)

    def ag_copy(k, d, source):
        return pltpu.make_async_remote_copy(
            src_ref=ag[k].at[me], dst_ref=ag[k].at[source], send_sem=ag_s.at[k * n + d], recv_sem=ag_r.at[k * n + d],
            device_id={"slab": lax.rem(me + d, n)}, device_id_type=MESH)

    def forward(k, d):
        source = lax.rem(me + n - d, n)
        return pltpu.make_async_remote_copy(
            src_ref=ag[k].at[source], dst_ref=other[k].at[source], send_sem=fwd_s.at[k * n + d], recv_sem=fwd_r.at[k * n + d],
            device_id={"pencil": mate}, device_id_type=MESH)

    partner = me + 1 - 2 * lax.rem(me, 2)

    def stride_copy(d, source):
        return pltpu.make_async_remote_copy(
            src_ref=ag[0].at[me], dst_ref=ag[0].at[source], send_sem=ag_s.at[d], recv_sem=ag_r.at[d],
            device_id={"slab": lax.rem(me + 2 * d, n)}, device_id_type=MESH)

    def relay_copy(d, landing):
        return pltpu.make_async_remote_copy(
            src_ref=ag[0].at[lax.rem(me + n - 2 * d, n)], dst_ref=ag[0].at[landing], send_sem=ag_s.at[n // 2 + d], recv_sem=ag_r.at[n // 2 + d],
            device_id={"slab": partner}, device_id_type=MESH)

    def relay(d, carry):
        source = lax.rem(me + n - 2 * d, n)
        stride_copy(d, source).wait()
        relay_copy(d, source).start()
        return carry

    def relayed(d, carry):
        relay_copy(d, lax.rem(partner + n - 2 * d, n)).wait()
        return carry

    def begin(k):
        for p in range(3):
            if pieces[p][0] == k:
                pair(p).wait_recv()
        total = sums[k][pen] + xbuf[k][...]
        for s in range(n):
            chunks[k][s] = total[s * rows:(s + 1) * rows].astype(RS_T)
        far_first(lambda d: rs_copy(k, d).start())

    def finish(k):
        each(lambda d: rs_copy(k, d).wait())
        mine = chunks[k][me].astype(F32)
        mine = lax.fori_loop(1, n, lambda d, acc: acc + rs[k][d].astype(F32), mine)
        ag[k][me] = mine.astype(AG_T)
        if k == 0:
            lax.fori_loop(1, n // 2, lambda d, c: stride_copy(d, me).start() or c, 0)
            relay_copy(0, me).start()
        else:
            far_first(lambda d: ag_copy(k, d, me).start())
        if k > 0:
            forward(k, 0).start()

    def collect(k):
        if k == 0:
            lax.fori_loop(1, n // 2, relay, 0)
            lax.fori_loop(0, n // 2, relayed, 0)
            whole = pltpu.make_async_remote_copy(
                src_ref=ag[k], dst_ref=other[k], send_sem=fwd_s.at[0], recv_sem=fwd_r.at[0],
                device_id={"pencil": mate}, device_id_type=MESH)
            whole.start()
            return whole
        forward(k, 0).wait()
        each(lambda d: forward(k, d).wait())

    def pass_on(k, d):
        ag_copy(k, d, lax.rem(me + n - d, n)).wait()
        forward(k, d).start()

    def second_block(tz, ty):
        i, z = {1: (0, 0), 2: (0, 1), 0: (1, 1)}[tz]
        at = {1: ((0, 0), (1, 2)), 2: ((0, 1), (1, 3)), 0: ((1, 1), (2, 3))}[ty]
        left = cat([up[i, j] for j, y in at], 1)
        right = cat([hid[z, y] for j, y in at], 1)
        block = dot(left, right, 1, 1)
        return [block[tx * 64:(tx + 1) * 64] for tx in range(3)]

    def first_block(i, tz):
        cells = cat([grad[i, j, 0:64, :] for j in range(4)], 1)
        taps = cat([patch(i, j, tz) for j in range(4)], 1)
        return dot(cells, taps, 1, 1)

    inner_plane()
    taps_0 = [t for ty in range(3) for t in second_block(0, ty)]
    taps_2 = [t for ty in range(3) for t in second_block(2, ty)]
    sums_0[0] = cat(taps_0[:8], 1) * scales[1]
    sums_0[1] = cat(taps_2[:8], 1) * scales[1]
    pair(0).start()
    for tz in range(3):
        inner[tz] = first_block(1, tz)
    part_up.wait()
    part_up0.wait()
    face_plane(0, down_own, up_in)
    begin(0)
    part_down.wait()
    part_down0.wait()
    face_plane(2, up_own, down_in)
    low = pl.ds(0, 64)
    grad_y = send(grad.at[pl.ds(0, 3), 0, low], grad.at[pl.ds(0, 3), 4, low], 8, me, mate)

    taps_1 = [t for ty in range(3) for t in second_block(1, ty)]
    pad = jnp.zeros((64, 64), F32)
    sums_1[0, :, 512:896] = cat(taps_0[8:] + taps_1[:5], 1) * scales[1]
    sums_1[1, :, 512:896] = cat(taps_1[5:] + taps_2[8:] + [pad], 1) * scales[1]
    near = (inner[1] + first_block(0, 1)) * scales[0]
    last = (inner[2] + first_block(0, 2)) * scales[0]
    sums_1[0, :, 0:512] = near[:, 64:]
    sums_1[1, :, 0:512] = last[:, :512]
    pair(1).start()
    base = (inner[0] + first_block(2, 0)) * scales[0]
    sums_1[0, :, 896:1280] = base[:, :384]
    sums_1[1, :, 896:1280] = cat([base[:, 384:], near[:, :64], last[:, 512:], pad], 1)
    pair(2).start()
    begin(1)
    pair(0).wait_send()
    pair(1).wait_send()
    pair(2).wait_send()

    grad_y.wait()
    for i, j in [(0, 4), (1, 4), (2, 4)]:
        here = grad[i, j, 0:64, :].astype(F32)
        grad[i, j, 64:128, :] = pltpu.roll(here, 127, 1).astype(BF16)

    def spread_plane(i):
        rhs = cat([cat([grad[i + a, j + b] for j in range(4)], 1) for a in range(2) for b in range(2)], 0)
        res = dot(wq[...], rhs, 0, 0)
        for pz in range(2):
            for py in range(2):
                for px in range(2):
                    m = ((pz * 2 + py) * 2 + px) * 64
                    for j in range(4):
                        at = pl.ds((2 * i + pz) * 8 + 2 * j + py, 64, stride=32)
                        xs[px, at, :] = res[m:m + 64, j * 128:(j + 1) * 128]

    join = select_matrix(256, 256, lambda r, c: c == jnp.where(r < 128, 2 * r, 2 * r - 255))

    spread_plane(0)
    spread_plane(1)
    finish(0)
    both = cat([xs[0].astype(BF16), xs[1].astype(BF16)], 1)
    fg_ref[...] = dot(both, join, 1, 0).astype(BF16)

    finish(1)
    places = (
        ((0, 0, 512, 1, 0), (1, 0, 512, 1, 1152)),
        ((0, 0, 512, 0, 640), (1, 0, 512, 0, 1152), (0, 512, 384, 1, 512), (1, 512, 256, 1, 896), (1, 768, 64, 1, 1664),
         (0, 896, 384, 0, 0), (1, 896, 256, 0, 384), (1, 1152, 64, 0, 1664)),
    )
    whole = collect(0)
    each(lambda d: pass_on(1, d))
    for k in range(2):
        whole.wait() if k == 0 else collect(1)
        for owner, begins, size, g, to in places[k]:
            for s in range(n):
                own, far = ag[k][s, :, begins:begins + size].astype(F32), other[k][s, :, begins:begins + size].astype(F32)
                (g1_ref, g2_ref)[g][s * rows:(s + 1) * rows, to:to + size] = jnp.where(pen == owner, own, far)


def store(fg, g1, g2, fg_hbm, g1_hbm, g2_hbm, sem):
    pairs = ((fg, fg_hbm), (g1, g1_hbm), (g2, g2_hbm))
    copies = [pltpu.make_async_copy(a, b, sem.at[k]) for k, (a, b) in enumerate(pairs)]
    for copy in copies:
        copy.start()
    for copy in copies:
        copy.wait()


def local(fine_field, coarse_cotangent, first_weight, second_weight):
    n, npen = lax.axis_size("slab"), lax.axis_size("pencil")
    members = n * npen
    scales = (1.0 / math.sqrt(1024 * members), 1.0 / math.sqrt(128 * members))
    rows = 64 // n
    widths = (512, 1280)
    vmem = pl.BlockSpec(memory_space=pltpu.VMEM)
    hbm = pl.BlockSpec(memory_space=pltpu.HBM)
    dma = pltpu.SemaphoreType.DMA
    outs = (
        jax.ShapeDtypeStruct((2048, 256), BF16),
        jax.ShapeDtypeStruct((64, 1728), F32),
        jax.ShapeDtypeStruct((64, 1728), F32),
    )
    held = (pltpu.VMEM((2048, 256), BF16), pltpu.VMEM((64, 1728), F32), pltpu.VMEM((64, 1728), F32))
    operands = (fine_field.reshape(2048, 256), coarse_cotangent.reshape(128, 64), first_weight, second_weight)
    results = pl.pallas_call(
        functools.partial(kernel, n, npen, scales),
        out_shape=held,
        in_specs=[hbm] * 4,
        out_specs=(vmem, vmem, vmem),
        scratch_shapes=[
            pltpu.VMEM((2048, 256), BF16),
            pltpu.VMEM((128, 64), BF16),
            pltpu.VMEM((64, 1728), BF16),
            pltpu.VMEM((64, 1728), BF16),
            dma((4,)),
            pltpu.VMEM((2, 2048, 128), F32),
            pltpu.VMEM((4, 9, 192, 128), BF16),
            *[pltpu.VMEM((256, 128), BF16), pltpu.VMEM((256, 128), BF16), pltpu.VMEM((256, 128), F32)] * 2,
            pltpu.VMEM((3, 64, 576), F32),
            pltpu.VMEM((2, 3, 192, 128), BF16),
            pltpu.VMEM((3, 5, 128, 128), BF16),
            pltpu.VMEM((2, 4, 64, 128), BF16),
            pltpu.VMEM((128, 128), F32),
            pltpu.VMEM((512, 512), BF16),
            pltpu.VMEM((768, 256), BF16),
            *[pltpu.VMEM((2, 64, w), F32) for w in widths],
            *[pltpu.VMEM((64, w), F32) for w in widths],
            *[pltpu.VMEM((n, rows, w), RS_T) for w in widths],
            *[pltpu.VMEM((n, rows, w), RS_T) for w in widths],
            *[pltpu.VMEM((n, rows, w), AG_T) for w in widths],
            *[pltpu.VMEM((n, rows, w), AG_T) for w in widths],
            dma((11,)), dma((11,)), dma((2 * n,)), dma((2 * n,)), dma((2 * n,)), dma((2 * n,)), dma((3,)), dma((3,)), dma((2 * n,)), dma((2 * n,)),
        ],
        compiler_params=pltpu.CompilerParams(
            collective_id=0, has_side_effects=True, vmem_limit_bytes=40 * 1024 * 1024),
    )(*[pltpu.with_memory_space_constraint(v, pltpu.HBM) for v in operands])
    results = [pltpu.with_memory_space_constraint(v, pltpu.VMEM) for v in results]
    fine_grad, first_grad, second_grad = pl.pallas_call(
        store,
        out_shape=outs,
        in_specs=[vmem] * 3,
        out_specs=(hbm,) * 3,
        scratch_shapes=[dma((3,))],
    )(*results)
    return fine_grad.reshape(fine_field.shape), first_grad, second_grad


def solution(mesh):
    placed = (P("groups", "slab", "pencil", None), P("groups", "slab", "pencil", None), P(), P())
    return jax.shard_map(
        local,
        mesh=mesh,
        in_specs=placed,
        out_specs=(P("groups", "slab", "pencil", None), P("groups", None), P("groups", None)),
        check_vma=False,
    )
```

```python
import functools
import math

import jax
import jax.numpy as jnp
from jax import lax
from jax.experimental import pallas as pl
from jax.experimental.pallas import tpu as pltpu
from jax.sharding import PartitionSpec as P

MESH = pl.DeviceIdType.MESH
F32, BF16 = jnp.float32, jnp.bfloat16
RS_T, AG_T = BF16, BF16
TAP = {(0, 0): 1, (1, 0): 2, (1, 1): 0}


def tap(parity, off):
    return TAP.get((parity, off))


def dot(a, b, da, db):
    return lax.dot_general(a, b, (((da,), (db,)), ((), ())), preferred_element_type=F32)


def cat(parts, axis):
    return jnp.concatenate(parts, axis=axis)


def select_matrix(rows, columns, fn):
    row = lax.broadcasted_iota(jnp.int32, (rows, columns), 0)
    col = lax.broadcasted_iota(jnp.int32, (rows, columns), 1)
    return jnp.where(fn(row, col), 1.0, 0.0).astype(BF16)


def kernel(n, npen, scales, x_hbm, cot_hbm, w1_hbm, w2_hbm, fg_ref, g1_ref, g2_ref,
           x_ref, cot_ref, w1_ref, w2_ref, in_sem, xs, fine, up_out, up_in, up_own, down_out, down_in, down_own, inner, up, grad, hid, cs, wq, w2q, sums_0, sums_1, xbuf_0, xbuf_1, chunks_0, chunks_1, rs_0, rs_1, ag_0, ag_1, other_0, other_1,
           halo_s, halo_r, rs_s, rs_r, ag_s, ag_r, pair_s, pair_r, fwd_s, fwd_r):
    me = lax.axis_index("slab")
    pen = lax.axis_index("pencil")
    above = lax.rem(me + 1, n)
    below = lax.rem(me + n - 1, n)
    mate = lax.rem(pen + 1, npen)
    rows = 64 // n

    barrier = pltpu.get_barrier_semaphore()

    def greet(s, p):
        pl.semaphore_signal(barrier, inc=1, device_id={"slab": s, "pencil": p}, device_id_type=MESH)

    def greet_peer(d, carry):
        greet(lax.rem(me + d, n), pen)
        return carry

    cot_in = pltpu.make_async_copy(cot_hbm, cot_ref, in_sem.at[0])
    cot_in.start()
    x_in = pltpu.make_async_copy(x_hbm, x_ref, in_sem.at[3])
    x_in.start()
    w1_in = pltpu.make_async_copy(w1_hbm, w1_ref, in_sem.at[1])
    w1_in.start()
    w2_in = pltpu.make_async_copy(w2_hbm, w2_ref, in_sem.at[2])
    w2_in.start()

    lax.fori_loop(1, n, greet_peer, 0)
    greet(me, mate)
    greet(above, mate)
    greet(below, mate)

    def send(src, dst, k, s, p):
        copy = pltpu.make_async_remote_copy(
            src_ref=src, dst_ref=dst, send_sem=halo_s.at[k], recv_sem=halo_r.at[k],
            device_id={"slab": s, "pencil": p}, device_id_type=MESH)
        copy.start()
        return copy

    spread = select_matrix(64, 128, lambda r, c: c == 2 * r)
    cot_in.wait()
    cs[...] = dot(cot_ref[...], spread, 1, 0)
    for j in range(2):
        up[0, j, 64:128, :] = cs[pl.ds(j, 64, stride=2), :].astype(BF16)

    split = select_matrix(256, 256, lambda r, c: r == jnp.where(c < 128, 2 * c, 2 * c - 255))

    x_in.wait()
    both = dot(x_ref[...], split, 1, 0)
    xs[0] = both[:, :128]
    xs[1] = both[:, 128:]

    def plane(z, y):
        at = pl.ds(z * 8 + y, 64, stride=32)
        even, odd = xs[0, at, :], xs[1, at, :]
        fine[z, y + 1, 64:128, :] = even.astype(BF16)
        fine[z, y + 1, 128:192, :] = odd.astype(BF16)
        fine[z, y + 1, 0:64, :] = pltpu.roll(odd, 1, 1).astype(BF16)

    def rim_send(z, count, k):
        at = pl.ds(z, count)
        return send(fine.at[at, 8, halves], fine.at[at, 0, halves], k, me, mate)

    def rim(z):
        odd = fine[z, 0, 128:192, :].astype(F32)
        fine[z, 0, 0:64, :] = pltpu.roll(odd, 1, 1).astype(BF16)

    def column(z, j):
        return fine[z, 2 * j:2 * j + 3].reshape(576, 128)

    def partial_sum(own, out, landing, k, to, planes, weight, first):
        at = slice(0, 1) if first else slice(1, 4)
        taps = cat([cat([column(z, j) for j in range(4)[at]], 1) for z in planes], 0)
        res = dot(weight, taps, 1, 0)
        piece = pl.ds(0, 64) if first else pl.ds(64, 192)
        for j in range(4)[at]:
            c = res[:, (j - at.start) * 128:(j - at.start + 1) * 128]
            own[j * 64:(j + 1) * 64] = c
            out[j * 64:(j + 1) * 64] = c.astype(BF16)
        return send(out.at[piece], landing.at[piece], k, to, pen)

    for y in range(8):
        plane(3, y)
    pl.semaphore_wait(barrier, n + 2)
    halves = pl.ds(64, 128)
    middle = pl.ds(64, 64)
    up_z = send(up.at[0, pl.ds(0, 2), middle], up.at[1, pl.ds(0, 2), middle], 0, below, pen)
    up_y = send(up.at[0, 0, middle], up.at[0, 2, middle], 1, me, mate)
    up_c = send(up.at[0, 0, middle], up.at[1, 2, middle], 2, below, mate)
    rim_3 = rim_send(3, 1, 3)
    w1_in.wait()
    part_up = partial_sum(up_own, up_out, up_in, 4, above, (3,), w1_ref[:, 0:576], False)
    plane(0, 7)
    plane(1, 7)
    rim_01 = rim_send(0, 2, 5)
    for z in range(2):
        for y in range(7):
            plane(z, y)
    part_down = partial_sum(down_own, down_out, down_in, 6, below, (0, 1), w1_ref[:, 576:], False)
    plane(2, 7)
    rim_2 = rim_send(2, 1, 7)
    rim_3.wait()
    rim(3)
    part_up0 = partial_sum(up_own, up_out, up_in, 9, above, (3,), w1_ref[:, 0:576], True)
    rim_01.wait()
    rim(0)
    rim(1)
    part_down0 = partial_sum(down_own, down_out, down_in, 10, below, (0, 1), w1_ref[:, 576:], True)
    for y in range(7):
        plane(2, y)

    w2_in.wait()
    wq[...] = jnp.zeros_like(wq)
    w2q[...] = jnp.zeros_like(w2q)
    for a in range(2):
        for b in range(2):
            for pz in range(2):
                for py in range(2):
                    tz, ty = tap(pz, a), tap(py, b)
                    if tz is None or ty is None:
                        continue
                    for tx in range(3):
                        t = ((tz * 3 + ty) * 3 + tx) * 64
                        px, r = {1: (0, 0), 2: (1, 0), 0: (1, 1)}[tx]
                        k = ((a * 2 + b) * 2 + r) * 64
                        m = ((pz * 2 + py) * 2 + px) * 64
                        wq[k:k + 64, m:m + 64] = w1_ref[:, t:t + 64]
                        k2 = ((a * 2 + b) * 3 + tx) * 64
                        m2 = (pz * 2 + py) * 64
                        w2q[k2:k2 + 64, m2:m2 + 64] = w2_ref[:, t:t + 64]

    up_z.wait()
    up_y.wait()
    up_c.wait()
    for i in range(2):
        for j in range(3):
            mid = up[i, j, 64:128, :].astype(F32)
            up[i, j, 0:64, :] = pltpu.roll(mid, 127, 1).astype(BF16)
            up[i, j, 128:192, :] = pltpu.roll(mid, 1, 1).astype(BF16)
    rhs = cat([cat([up[a, j + b] for j in range(2)], 1) for a in range(2) for b in range(2)], 0)
    hidden_grad = dot(w2q[...], rhs, 0, 0)
    rhs = cat([cat([up[1, j + b] for j in range(2)], 1) for b in range(2)], 0)
    hidden_above = dot(w2q[0:384, 0:128], rhs, 0, 0)

    rim_2.wait()
    rim(2)

    def patch(i, j, tz):
        return fine[2 * i + tz - 1, 2 * j:2 * j + 3].reshape(576, 128)

    def middle_row(i, y, act):
        sig = jax.nn.sigmoid(act)
        if i < 2:
            hid[i, y] = (act * sig).astype(BF16)
        m = (i % 2 * 2 + y % 2) * 64
        back = (hidden_above if i == 2 else hidden_grad)[m:m + 64, (y // 2) * 128:(y // 2 + 1) * 128]
        pre_grad = (back * (sig * (1.0 + act * (1.0 - sig)))).astype(BF16)
        grad[i, y, 0:64, :] = pre_grad
        grad[i, y, 64:128, :] = pltpu.roll(pre_grad.astype(F32), 127, 1).astype(BF16)

    def inner_plane():
        taps = cat([cat([patch(1, j, tz) for j in range(4)], 1) for tz in range(3)], 0)
        pre_act = dot(w1_ref[...], taps, 1, 0)
        for y in range(4):
            middle_row(1, y, pre_act[:, y * 128:(y + 1) * 128])

    def face_plane(i, own, far):
        for y in range(4):
            at = slice(y * 64, (y + 1) * 64)
            middle_row(i, y, own[at] + far[at].astype(F32))

    def each(fn):
        def body(d, carry):
            fn(d)
            return carry

        lax.fori_loop(1, n, body, 0)

    def far_first(fn):
        def body(k, carry):
            down, up = n - k, k - 1
            down = jnp.where(down > me, down, down - 1)
            up = jnp.where(up < me, up, up + 1)
            fn(lax.rem(jnp.where(2 * me < n, down, up) + n - me, n))
            return carry

        lax.fori_loop(1, n, body, 0)

    sums, xbuf, chunks = (sums_0, sums_1), (xbuf_0, xbuf_1), (chunks_0, chunks_1)
    rs, ag, other = (rs_0, rs_1), (ag_0, ag_1), (other_0, other_1)

    pieces = ((0, 0, 512), (1, 0, 896), (1, 896, 384))

    def pair(p):
        k, begins, size = pieces[p]
        at = pl.ds(begins, size)
        return pltpu.make_async_remote_copy(
            src_ref=sums[k].at[1 - pen, :, at], dst_ref=xbuf[k].at[:, at], send_sem=pair_s.at[p], recv_sem=pair_r.at[p],
            device_id={"pencil": mate}, device_id_type=MESH)

    def rs_copy(k, d):
        to = lax.rem(me + d, n)
        return pltpu.make_async_remote_copy(
            src_ref=chunks[k].at[to], dst_ref=rs[k].at[d], send_sem=rs_s.at[k * n + d], recv_sem=rs_r.at[k * n + d],
            device_id={"slab": to}, device_id_type=MESH)

    def ag_copy(k, d, source):
        return pltpu.make_async_remote_copy(
            src_ref=ag[k].at[me], dst_ref=ag[k].at[source], send_sem=ag_s.at[k * n + d], recv_sem=ag_r.at[k * n + d],
            device_id={"slab": lax.rem(me + d, n)}, device_id_type=MESH)

    def forward(k, d):
        source = lax.rem(me + n - d, n)
        return pltpu.make_async_remote_copy(
            src_ref=ag[k].at[source], dst_ref=other[k].at[source], send_sem=fwd_s.at[k * n + d], recv_sem=fwd_r.at[k * n + d],
            device_id={"pencil": mate}, device_id_type=MESH)

    partner = me + 1 - 2 * lax.rem(me, 2)

    def stride_copy(d, source):
        return pltpu.make_async_remote_copy(
            src_ref=ag[0].at[me], dst_ref=ag[0].at[source], send_sem=ag_s.at[d], recv_sem=ag_r.at[d],
            device_id={"slab": lax.rem(me + 2 * d, n)}, device_id_type=MESH)

    def relay_copy(d, landing):
        return pltpu.make_async_remote_copy(
            src_ref=ag[0].at[lax.rem(me + n - 2 * d, n)], dst_ref=ag[0].at[landing], send_sem=ag_s.at[n // 2 + d], recv_sem=ag_r.at[n // 2 + d],
            device_id={"slab": partner}, device_id_type=MESH)

    def relay(d, carry):
        source = lax.rem(me + n - 2 * d, n)
        stride_copy(d, source).wait()
        relay_copy(d, source).start()
        return carry

    def relayed(d, carry):
        relay_copy(d, lax.rem(partner + n - 2 * d, n)).wait()
        return carry

    def begin(k):
        for p in range(3):
            if pieces[p][0] == k:
                pair(p).wait_recv()
        total = sums[k][pen] + xbuf[k][...]
        for s in range(n):
            chunks[k][s] = total[s * rows:(s + 1) * rows].astype(RS_T)
        far_first(lambda d: rs_copy(k, d).start())

    def finish(k):
        each(lambda d: rs_copy(k, d).wait())
        mine = chunks[k][me].astype(F32)
        mine = lax.fori_loop(1, n, lambda d, acc: acc + rs[k][d].astype(F32), mine)
        ag[k][me] = mine.astype(AG_T)
        if k == 0:
            lax.fori_loop(1, n // 2, lambda d, c: stride_copy(d, me).start() or c, 0)
            relay_copy(0, me).start()
        else:
            far_first(lambda d: ag_copy(k, d, me).start())
        if k > 0:
            forward(k, 0).start()

    def collect(k):
        if k == 0:
            lax.fori_loop(1, n // 2, relay, 0)
            lax.fori_loop(0, n // 2, relayed, 0)
            whole = pltpu.make_async_remote_copy(
                src_ref=ag[k], dst_ref=other[k], send_sem=fwd_s.at[0], recv_sem=fwd_r.at[0],
                device_id={"pencil": mate}, device_id_type=MESH)
            whole.start()
            return whole
        forward(k, 0).wait()
        each(lambda d: forward(k, d).wait())

    def pass_on(k, d):
        ag_copy(k, d, lax.rem(me + n - d, n)).wait()
        forward(k, d).start()

    def second_block(tz, ty):
        i, z = {1: (0, 0), 2: (0, 1), 0: (1, 1)}[tz]
        at = {1: ((0, 0), (1, 2)), 2: ((0, 1), (1, 3)), 0: ((1, 1), (2, 3))}[ty]
        left = cat([up[i, j] for j, y in at], 1)
        right = cat([hid[z, y] for j, y in at], 1)
        block = dot(left, right, 1, 1)
        return [block[tx * 64:(tx + 1) * 64] for tx in range(3)]

    def first_block(i, tz):
        cells = cat([grad[i, j, 0:64, :] for j in range(4)], 1)
        taps = cat([patch(i, j, tz) for j in range(4)], 1)
        return dot(cells, taps, 1, 1)

    inner_plane()
    taps_0 = [t for ty in range(3) for t in second_block(0, ty)]
    taps_2 = [t for ty in range(3) for t in second_block(2, ty)]
    sums_0[0] = cat(taps_0[:8], 1) * scales[1]
    sums_0[1] = cat(taps_2[:8], 1) * scales[1]
    pair(0).start()
    for tz in range(3):
        inner[tz] = first_block(1, tz)
    part_up.wait()
    part_up0.wait()
    face_plane(0, down_own, up_in)
    begin(0)
    part_down.wait()
    part_down0.wait()
    face_plane(2, up_own, down_in)
    low = pl.ds(0, 64)
    grad_y = send(grad.at[pl.ds(0, 3), 0, low], grad.at[pl.ds(0, 3), 4, low], 8, me, mate)

    taps_1 = [t for ty in range(3) for t in second_block(1, ty)]
    pad = jnp.zeros((64, 64), F32)
    sums_1[0, :, 512:896] = cat(taps_0[8:] + taps_1[:5], 1) * scales[1]
    sums_1[1, :, 512:896] = cat(taps_1[5:] + taps_2[8:] + [pad], 1) * scales[1]
    near = (inner[1] + first_block(0, 1)) * scales[0]
    last = (inner[2] + first_block(0, 2)) * scales[0]
    sums_1[0, :, 0:512] = near[:, 64:]
    sums_1[1, :, 0:512] = last[:, :512]
    pair(1).start()
    base = (inner[0] + first_block(2, 0)) * scales[0]
    sums_1[0, :, 896:1280] = base[:, :384]
    sums_1[1, :, 896:1280] = cat([base[:, 384:], near[:, :64], last[:, 512:], pad], 1)
    pair(2).start()
    begin(1)
    pair(0).wait_send()
    pair(1).wait_send()
    pair(2).wait_send()

    grad_y.wait()
    for i, j in [(0, 4), (1, 4), (2, 4)]:
        here = grad[i, j, 0:64, :].astype(F32)
        grad[i, j, 64:128, :] = pltpu.roll(here, 127, 1).astype(BF16)

    def spread_plane(i):
        rhs = cat([cat([grad[i + a, j + b] for j in range(4)], 1) for a in range(2) for b in range(2)], 0)
        res = dot(wq[...], rhs, 0, 0)
        for pz in range(2):
            for py in range(2):
                for px in range(2):
                    m = ((pz * 2 + py) * 2 + px) * 64
                    for j in range(4):
                        at = pl.ds((2 * i + pz) * 8 + 2 * j + py, 64, stride=32)
                        xs[px, at, :] = res[m:m + 64, j * 128:(j + 1) * 128]

    join = select_matrix(256, 256, lambda r, c: c == jnp.where(r < 128, 2 * r, 2 * r - 255))

    spread_plane(0)
    spread_plane(1)
    finish(0)
    both = cat([xs[0].astype(BF16), xs[1].astype(BF16)], 1)
    fg_ref[...] = dot(both, join, 1, 0).astype(BF16)

    finish(1)
    places = (
        ((0, 0, 512, 1, 0), (1, 0, 512, 1, 1152)),
        ((0, 0, 512, 0, 640), (1, 0, 512, 0, 1152), (0, 512, 384, 1, 512), (1, 512, 256, 1, 896), (1, 768, 64, 1, 1664),
         (0, 896, 384, 0, 0), (1, 896, 256, 0, 384), (1, 1152, 64, 0, 1664)),
    )
    whole = collect(0)
    each(lambda d: pass_on(1, d))
    for k in range(2):
        whole.wait() if k == 0 else collect(1)
        for owner, begins, size, g, to in places[k]:
            for s in range(n):
                own, far = ag[k][s, :, begins:begins + size].astype(F32), other[k][s, :, begins:begins + size].astype(F32)
                (g1_ref, g2_ref)[g][s * rows:(s + 1) * rows, to:to + size] = jnp.where(pen == owner, own, far)


def store(fg, g1, g2, fg_hbm, g1_hbm, g2_hbm, sem):
    pairs = ((fg, fg_hbm), (g1, g1_hbm), (g2, g2_hbm))
    copies = [pltpu.make_async_copy(a, b, sem.at[k]) for k, (a, b) in enumerate(pairs)]
    for copy in copies:
        copy.start()
    for copy in copies:
        copy.wait()


def local(fine_field, coarse_cotangent, first_weight, second_weight):
    n, npen = lax.axis_size("slab"), lax.axis_size("pencil")
    members = n * npen
    scales = (1.0 / math.sqrt(1024 * members), 1.0 / math.sqrt(128 * members))
    rows = 64 // n
    widths = (512, 1280)
    vmem = pl.BlockSpec(memory_space=pltpu.VMEM)
    hbm = pl.BlockSpec(memory_space=pltpu.HBM)
    dma = pltpu.SemaphoreType.DMA
    outs = (
        jax.ShapeDtypeStruct((2048, 256), BF16),
        jax.ShapeDtypeStruct((64, 1728), F32),
        jax.ShapeDtypeStruct((64, 1728), F32),
    )
    held = (pltpu.VMEM((2048, 256), BF16), pltpu.VMEM((64, 1728), F32), pltpu.VMEM((64, 1728), F32))
    operands = (fine_field.reshape(2048, 256), coarse_cotangent.reshape(128, 64), first_weight, second_weight)
    results = pl.pallas_call(
        functools.partial(kernel, n, npen, scales),
        out_shape=held,
        in_specs=[hbm] * 4,
        out_specs=(vmem, vmem, vmem),
        scratch_shapes=[
            pltpu.VMEM((2048, 256), BF16),
            pltpu.VMEM((128, 64), BF16),
            pltpu.VMEM((64, 1728), BF16),
            pltpu.VMEM((64, 1728), BF16),
            dma((4,)),
            pltpu.VMEM((2, 2048, 128), F32),
            pltpu.VMEM((4, 9, 192, 128), BF16),
            *[pltpu.VMEM((256, 128), BF16), pltpu.VMEM((256, 128), BF16), pltpu.VMEM((256, 128), F32)] * 2,
            pltpu.VMEM((3, 64, 576), F32),
            pltpu.VMEM((2, 3, 192, 128), BF16),
            pltpu.VMEM((3, 5, 128, 128), BF16),
            pltpu.VMEM((2, 4, 64, 128), BF16),
            pltpu.VMEM((128, 128), F32),
            pltpu.VMEM((512, 512), BF16),
            pltpu.VMEM((768, 256), BF16),
            *[pltpu.VMEM((2, 64, w), F32) for w in widths],
            *[pltpu.VMEM((64, w), F32) for w in widths],
            *[pltpu.VMEM((n, rows, w), RS_T) for w in widths],
            *[pltpu.VMEM((n, rows, w), RS_T) for w in widths],
            *[pltpu.VMEM((n, rows, w), AG_T) for w in widths],
            *[pltpu.VMEM((n, rows, w), AG_T) for w in widths],
            dma((11,)), dma((11,)), dma((2 * n,)), dma((2 * n,)), dma((2 * n,)), dma((2 * n,)), dma((3,)), dma((3,)), dma((2 * n,)), dma((2 * n,)),
        ],
        compiler_params=pltpu.CompilerParams(
            collective_id=0, has_side_effects=True, vmem_limit_bytes=40 * 1024 * 1024),
    )(*[pltpu.with_memory_space_constraint(v, pltpu.HBM) for v in operands])
    results = [pltpu.with_memory_space_constraint(v, pltpu.VMEM) for v in results]
    fine_grad, first_grad, second_grad = pl.pallas_call(
        store,
        out_shape=outs,
        in_specs=[vmem] * 3,
        out_specs=(hbm,) * 3,
        scratch_shapes=[dma((3,))],
    )(*results)
    return fine_grad.reshape(fine_field.shape), first_grad, second_grad


def solution(mesh):
    placed = (P("groups", "slab", "pencil", None), P("groups", "slab", "pencil", None), P(), P())
    return jax.shard_map(
        local,
        mesh=mesh,
        in_specs=placed,
        out_specs=(P("groups", "slab", "pencil", None), P("groups", None), P("groups", None)),
        check_vma=False,
    )
```
